256 devices in a mesh: fde: 8 (over z), pas: 32 (over x, y, core).
Axes of the slice: x: 4, y: 4, z: 8, core: 2. Of those that a mesh axis runs over, the one named last changes fastest.
Arguments:
- query_fixed_encoding: bfloat16 [128, 10240], P(None, 'fde'), may hold values from -6 to 6
- passage_fde: bfloat16 [8192, 10240], P('pas', 'fde'), may hold values from -0.0625 to 0.0625
- query_tokens: bfloat16 [128, 32, 128], P('fde'), may hold values from -6 to 6
- query_token_totals: int32 [128], P('fde'), may hold values from 1 to 32
- passage_tokens: bfloat16 [8192, 256, 128], P(('fde', 'pas')), may hold values from -0.5 to 0.5
- passage_lengths: int32 [8192], P(('fde', 'pas')), may hold values from 1 to 256
- candidates: int32 [128, 1024], P('fde', 'pas'), may hold values from 0 to 8191, as said below
Outputs:
- fde_scores: float32 [128, 8192], P('fde', 'pas')
- rerank: float32 [128, 1024], P('fde', 'pas')
The draws below stay inside these ranges and needn't reach their ends.
Inputs may be any that keep to these rules, and one draw needn't show every extreme that they name: Passage p is held by the device of linear index p // 32 over fde then pas. Among the 16 x 32 candidates held by one device, one quarter of the 256 devices (the same quarter for every device) is named exactly 6 times each, another quarter 2 times each, the rest not at all; within an owner device the ids are uniform and may repeat.
All inputs are finite; a program needn't handle non-finite values.
Results may differ from the reference program's by a relative error of at most 0.0003.
Values may be sent and summed in bfloat16 or wider, within the bound.
No kernel may reach another device: no remote copies, remote signals or barrier semaphores. Data moves between devices by JAX's collectives and lax.ppermute only.
A program may use at most 128 MiB of HBM per device.

```python
import jax
import jax.numpy as jnp
import numpy as np
from jax import lax

Q_DEV = 16
C_DEV = 32
F = 10240
DIM = 128
QT = 32
PT = 256
PASS_DEV = 32
Q = 128
CAND = 1024
OWNERS = 256
PASSAGES = 8192


def draw_candidates(key, part):
    quarter = OWNERS // 4
    mean_load = Q_DEV * C_DEV // OWNERS
    levels = np.concatenate([np.full(quarter, 3 * mean_load), np.full(quarter, mean_load), np.zeros(OWNERS - 2 * quarter)]).astype(np.int64)
    position = np.repeat(np.arange(OWNERS), levels).astype(np.int32)
    key_order, key_rest, key_local = jax.random.split(jax.random.fold_in(key, 17), 3)
    order = jax.random.permutation(key_order, jnp.arange(OWNERS, dtype=jnp.int32))
    hot_owners = order[:quarter]
    rare_passage_holders = order[quarter:]

    def one_source(source_key):
        key_cold, key_slots = jax.random.split(source_key)
        cold_mixed = jax.random.permutation(key_cold, rare_passage_holders)
        table = jnp.concatenate([hot_owners, cold_mixed])
        slot_order = jax.random.permutation(key_slots, jnp.asarray(position))
        return jnp.take(table, slot_order, axis=0)
    source_keys = jax.random.split(key_rest, OWNERS)
    owner_ids = jax.vmap(one_source)(source_keys)
    local_ids = jax.random.randint(key_local, (OWNERS, Q_DEV * C_DEV), 0, PASS_DEV, dtype=jnp.int32)
    passage_ids = owner_ids * PASS_DEV + local_ids
    groups = Q // Q_DEV
    shards = CAND // C_DEV
    arranged = passage_ids.reshape(groups, shards, Q_DEV, C_DEV)
    arranged = jnp.transpose(arranged, (0, 2, 1, 3)).reshape(Q, CAND)
    return arranged.astype(jnp.int32)


def with_ends(result, own_key, least, high):
    extent = result.shape
    index_at = [jax.random.randint(jax.random.fold_in(own_key, axis), (), 0, extent[axis]) for axis in range(len(extent))]
    result = result.at[tuple(index_at)].set(least)
    longest = extent.index(max(extent))
    index_at[longest] = (index_at[longest] + 1) % extent[longest]
    return result.at[tuple(index_at)].set(high)


def level_of(key, shape, cuts, least, top_value):
    def one(dim, parts):
        heights = jax.random.uniform(jax.random.fold_in(jax.random.fold_in(key, 6), dim), (parts,), jnp.float32, least / len(cuts), top_value / len(cuts))
        return jnp.repeat(jnp.exp(heights), shape[dim] // parts).reshape((-1,) + (1,) * (len(shape) - dim - 1))

    factor_of = one(*cuts[0])
    for cut in cuts[1:]:
        factor_of = factor_of * one(*cut)
    return factor_of


def bell_draw(own_key, shape, deviation, limit, pieces=(), held_as=jnp.bfloat16):
    drawn = deviation * jax.random.normal(own_key, shape, jnp.float32)
    if pieces:
        drawn = drawn * level_of(own_key, shape, pieces, -0.22, 0.18)
    return jnp.clip(drawn, -limit, limit).astype(held_as)


def setup_inputs(seed: int = 0) -> dict:
    splits = jax.random.split(jax.random.key(seed), 8)
    return {
        "query_fixed_encoding": bell_draw(splits[0], (Q, F), 1.0, 6.0, ((1, 8),)),
        "passage_fde": bell_draw(splits[1], (PASSAGES, F), F ** -0.5, 0.0625, ((0, 32), (1, 8))),
        "query_tokens": bell_draw(splits[2], (Q, QT, DIM), 1.0, 6.0, ((0, 8),)),
        "query_token_totals": with_ends(jax.random.randint(splits[3], (Q,), 1, QT + 1), jax.random.fold_in(splits[3], 1), 1, QT).astype(jnp.int32),
        "passage_tokens": bell_draw(splits[4], (PASSAGES, PT, DIM), DIM ** -0.5, 0.5, ((0, 256),)),
        "passage_lengths": with_ends(jax.random.randint(splits[5], (PASSAGES,), 1, PT + 1), jax.random.fold_in(splits[5], 1), 1, PT).astype(jnp.int32),
        "candidates": draw_candidates(jax.random.fold_in(splits[7], 71), 0),
    }


def reference(query_fixed_encoding, passage_fde, query_tokens, query_token_totals, passage_tokens, passage_lengths, candidates):
    query_wide = query_fixed_encoding.astype(jnp.float32)
    passage_blocks = passage_fde.reshape(OWNERS, PASS_DEV, F)

    def encode_block(block):
        return jnp.dot(query_wide, block.astype(jnp.float32).T, precision=lax.Precision.HIGHEST)

    block_scores = lax.map(encode_block, passage_blocks)
    fde_scores = jnp.transpose(block_scores, (1, 0, 2)).reshape(Q, PASSAGES)

    def per_query(inputs):
        token_vectors, count, passage_ids = inputs
        corpus_texts = jnp.take(passage_tokens, passage_ids, axis=0).astype(jnp.float32)
        lengths = jnp.take(passage_lengths, passage_ids, axis=0)
        similarity_matrix = jnp.einsum("jd,ctd->cjt", token_vectors.astype(jnp.float32), corpus_texts, precision=lax.Precision.HIGHEST)
        positions = jnp.arange(PT, dtype=jnp.int32)
        live = positions[None, None, :] < lengths[:, None, None]
        best_match = jnp.max(jnp.where(live, similarity_matrix, jnp.float32(-1e30)), axis=2)
        slots = jnp.arange(QT, dtype=jnp.int32)
        used = slots[None, :] < count
        summed = jnp.sum(jnp.where(used, best_match, jnp.float32(0.0)), axis=1)
        return summed / count.astype(jnp.float32)

    rerank = lax.map(per_query, (query_tokens, query_token_totals, candidates))
    return fde_scores, rerank
```

```python
import jax
import jax.numpy as jnp
from jax import lax
from jax.experimental import pallas as pl
from jax.experimental.pallas import tpu as pltpu
from jax.sharding import PartitionSpec as P

f32, bf16, i32 = jnp.float32, jnp.bfloat16, jnp.int32
NT = (((1,), (1,)), ((), ()))
NN = (((1,), (0,)), ((), ()))
VM = pl.BlockSpec(memory_space=pltpu.VMEM)
SM = pl.BlockSpec(memory_space=pltpu.SMEM)
CH = 64
GRP = 8
COLS = 512


def iota(shape, dim):
    return lax.broadcasted_iota(i32, shape, dim)


def split2(x):
    hi = x.astype(bf16)
    return hi, (x - hi.astype(f32)).astype(bf16)


def route_kernel(cand_ref, send_ref, meta_ref, hot_ref):
    nq, nc = cand_ref.shape
    n = nq * nc
    owners = hot_ref.shape[0]
    ids = jnp.concatenate([cand_ref[q : q + 1, :] for q in range(nq)], axis=1)
    owner, local = ids >> 5, ids & 31
    mine = iota((owners, n), 0) == owner
    hot = jnp.where(mine, 1.0, 0.0)
    hot_b = hot.astype(bf16)
    hot_ref[...] = hot_b
    earlier = jnp.where(iota((n, n), 0) < iota((n, n), 1), 1.0, 0.0).astype(bf16)
    before = lax.dot_general(hot_b, earlier, NN, preferred_element_type=f32)
    rank = jnp.sum(hot * before, axis=0, keepdims=True).astype(i32)
    here = iota((8, n), 0) == rank
    row = (iota((1, n), 1) // nc).astype(f32)
    vals = jnp.concatenate(
        [jnp.where(here, row, 0.0), jnp.where(here, local.astype(f32), 0.0)], axis=0
    ).astype(bf16)
    vals = jnp.concatenate([vals, jnp.zeros((112, n), bf16)], axis=0)
    table = lax.dot_general(hot_b, vals, NT, preferred_element_type=f32).astype(i32)
    moved = pltpu.roll(table, 120, 1)
    send_ref[...] = jnp.where(iota(table.shape, 1) < 8, table * 65536 + moved, 0)
    meta_ref[...] = jnp.broadcast_to(rank, meta_ref.shape)


def prep_kernel(len_ref, p_ref, o_ref, sched_ref):
    count, pt, dim = p_ref.shape
    per = pt // CH

    def clean(p, _):
        rows = p_ref[p].astype(f32)
        keep = iota((pt, dim), 0) < len_ref[p]
        o_ref[p] = jnp.where(keep, rows, rows[0:1, :]).astype(bf16)
        return 0

    lax.fori_loop(0, count, clean, 0, unroll=4)

    def listed(p, at):
        live = (len_ref[p] + (CH - 1)) // CH
        sched_ref[160 + p] = at
        sched_ref[192 + p] = live
        for k in range(per):
            sched_ref[at + k] = p * pt + k * CH
        return at + live

    total = lax.fori_loop(0, count, listed, 0)
    for k in range(GRP):
        sched_ref[total + k] = 0
    sched_ref[224] = (total + GRP - 1) // GRP


def best_matches(sched_ref, p_ref, q_ref, part_ref, best_ref):
    width = q_ref.shape[0]
    count = best_ref.shape[0]

    def step(g, _):
        rows = jnp.concatenate(
            [p_ref[pl.ds(pl.multiple_of(sched_ref[g * GRP + k], CH), CH), :] for k in range(GRP)],
            axis=0,
        )
        for c in range(width // COLS):
            sim = lax.dot_general(
                rows, q_ref[c * COLS : (c + 1) * COLS, :], NT, preferred_element_type=f32
            )
            m = jnp.max(sim.reshape(GRP, CH // 8, 8, COLS), axis=1)
            part_ref[pl.ds(pl.multiple_of(g * GRP * 8, GRP * 8), GRP * 8), c * COLS : (c + 1) * COLS] = (
                m.reshape(GRP * 8, COLS)
            )
        return 0

    lax.fori_loop(0, sched_ref[224], step, 0)

    def gather(p, _):
        at, live = sched_ref[160 + p], sched_ref[192 + p]
        m = None
        for k in range(256 // CH):
            c = at + jnp.minimum(k, live - 1)
            v = part_ref[pl.ds(pl.multiple_of(c * 8, 8), 8), :]
            m = v if m is None else jnp.maximum(m, v)
        best_ref[pl.ds(p, 1), :] = jnp.max(m, axis=0, keepdims=True)
        return 0

    lax.fori_loop(0, count, gather, 0)


def query_sums(best_ref):
    count, width = best_ref.shape
    hi, lo = split2(best_ref[...])
    nq = 128
    member = jnp.where(iota((nq, width), 1) // 32 == iota((nq, width), 0), 1.0, 0.0).astype(bf16)
    s = lax.dot_general(
        jnp.concatenate([hi, lo], axis=0), member, NT, preferred_element_type=f32
    )
    return s[:count] + s[count:]


def first_kernel(sched_ref, p_ref, q_ref, t_ref, part_ref, best_ref):
    best_matches(sched_ref, p_ref, q_ref, part_ref, best_ref)
    t_ref[...] = query_sums(best_ref)


def second_kernel(sched_ref, core_ref, p_ref, q_ref, ta_ref, req_ref, o_ref, part_ref, best_ref):
    best_matches(sched_ref, p_ref, q_ref, part_ref, best_ref)
    tb = query_sums(best_ref)
    ta = ta_ref[...]
    table = jnp.where(iota(ta.shape, 1) < 64, ta, pltpu.roll(tb, 64, 1))
    hi, lo = split2(table)
    table = jnp.concatenate([hi, lo], axis=0)
    req = req_ref[...]
    src = req.shape[0]
    q = req >> 16
    local = req & 65535
    half = (q >> 3) ^ core_ref[0]
    col = half * 64 + (iota(req.shape, 0) >> 5) * 8 + (q & 7)
    lane = iota(req.shape, 1)
    lane64 = iota((src, 64), 1) & 31
    out = jnp.zeros(req.shape, f32)
    for s in range(6):
        pick = jnp.where(lane == col[:, s : s + 1], 1.0, 0.0).astype(bf16)
        x = lax.dot_general(pick, table, NT, preferred_element_type=f32)
        x = jnp.sum(jnp.where(lane64 == local[:, s : s + 1], x, 0.0), axis=1, keepdims=True)
        out = jnp.where(lane == s, x, out)
    o_ref[...] = out


def final_kernel(count_ref, ret_ref, meta_ref, hot_ref, o_ref):
    nq, nc = o_ref.shape
    t = jnp.transpose(ret_ref[...])[:8, :]
    hi, lo = split2(t)
    x = lax.dot_general(
        jnp.concatenate([hi, lo], axis=0), hot_ref[...], NN, preferred_element_type=f32
    )
    x = x[:8] + x[8:]
    row = jnp.sum(jnp.where(iota(x.shape, 0) == meta_ref[...], x, 0.0), axis=0, keepdims=True)
    for q in range(nq):
        o_ref[q : q + 1, :] = row[:, q * nc : (q + 1) * nc] / count_ref[q].astype(f32)


def call(kernel, outs, ins, out_specs=VM, in_specs=None, scratch=(), name=None):
    return pl.pallas_call(
        kernel,
        out_shape=outs,
        in_specs=[VM] * len(ins) if in_specs is None else in_specs,
        out_specs=out_specs,
        scratch_shapes=scratch,
        name=name,
    )(*ins)


def body(
    query_fixed_encoding,
    passage_fde,
    query_tokens,
    query_token_totals,
    passage_tokens,
    passage_lengths,
    candidates,
):
    groups, shards = lax.axis_size("fde"), lax.axis_size("pas")
    owners = groups * shards
    nq, qt, dim = query_tokens.shape
    count, pt, _ = passage_tokens.shape
    core = lax.axis_index("pas") % 2
    S = jax.ShapeDtypeStruct

    live = iota((nq, qt, dim), 1) < query_token_totals[:, None, None]
    mine = jnp.where(live, query_tokens, jnp.zeros((), bf16)).reshape(2, nq * qt // 2, dim)
    mine = lax.dynamic_index_in_dim(mine, core, 0, keepdims=False)
    near = lax.all_to_all(
        jnp.broadcast_to(mine[None], (groups,) + mine.shape), "fde", 0, 0, tiled=True
    ).reshape(-1, dim)
    far = lax.ppermute(near, "pas", [(k, k ^ 1) for k in range(shards)])

    send, meta, hot = call(
        route_kernel,
        (S((owners, 128), i32), S((8, nq * candidates.shape[1]), i32), S((owners, nq * candidates.shape[1]), bf16)),
        (candidates,),
        (VM, VM, VM),
        name="route",
    )
    req = lax.all_to_all(send, ("fde", "pas"), 0, 0, tiled=True)

    clean, sched = call(
        prep_kernel,
        (S(passage_tokens.shape, bf16), S((256,), i32)),
        (passage_lengths, passage_tokens),
        (VM, SM),
        [SM, VM],
        name="prep",
    )
    clean = clean.reshape(count * pt, dim)

    partial = jnp.einsum(
        "qf,pf->qp", query_fixed_encoding, passage_fde, preferred_element_type=f32
    )
    tiles = lax.all_to_all(partial.reshape(groups, nq, -1), "fde", 0, 0, tiled=True)
    fde_scores = jnp.sum(tiles, axis=0)

    width = near.shape[0]
    scratch = [pltpu.VMEM((count * pt // CH * 8, width), f32), pltpu.VMEM((count, width), f32)]
    ta = call(
        first_kernel, S((count, 128), f32), (sched, clean, near), VM, [SM, VM, VM], scratch, "first"
    )
    resp = call(
        second_kernel,
        S((owners, 128), f32),
        (sched, core.reshape(1), clean, far, ta, req),
        VM,
        [SM, SM, VM, VM, VM, VM],
        scratch,
        "second",
    )
    ret = lax.all_to_all(resp, ("fde", "pas"), 0, 0, tiled=True)
    rerank = call(
        final_kernel,
        S(candidates.shape, f32),
        (query_token_totals, ret, meta[:1], hot),
        VM,
        [SM, VM, VM, VM],
        name="final",
    )
    return fde_scores, rerank


def solution(mesh):
    return jax.shard_map(
        body,
        mesh=mesh,
        in_specs=(
            P(None, "fde"),
            P("pas", "fde"),
            P("fde", None, None),
            P("fde"),
            P(("fde", "pas"), None, None),
            P(("fde", "pas")),
            P("fde", "pas"),
        ),
        out_specs=(P("fde", "pas"), P("fde", "pas")),
        check_vma=False,
    )
```

```python
import jax
import jax.numpy as jnp
from jax import lax
from jax.experimental import pallas as pl
from jax.experimental.pallas import tpu as pltpu
from jax.sharding import PartitionSpec as P


f32, bf16, i32 = jnp.float32, jnp.bfloat16, jnp.int32
NT = (((1,), (1,)), ((), ()))
TN = (((0,), (0,)), ((), ()))
VM = pl.BlockSpec(memory_space=pltpu.VMEM)
SM = pl.BlockSpec(memory_space=pltpu.SMEM)
CH = 64
GRP = 8
COLS = 512


def iota(shape, dim):
    return lax.broadcasted_iota(i32, shape, dim)


def split2(x):
    hi = x.astype(bf16)
    return hi, (x - hi.astype(f32)).astype(bf16)


def prep_kernel(len_ref, p_ref, o_ref, sched_ref):
    count, pt, dim = p_ref.shape
    per = pt // CH

    def clean(p, _):
        rows = p_ref[p].astype(f32)
        keep = iota((pt, dim), 0) < len_ref[p]
        o_ref[p] = jnp.where(keep, rows, rows[0:1, :]).astype(bf16)
        return 0

    lax.fori_loop(0, count, clean, 0, unroll=4)

    def listed(p, at):
        live = (len_ref[p] + (CH - 1)) // CH
        sched_ref[160 + p] = at
        sched_ref[192 + p] = live
        for k in range(per):
            sched_ref[at + k] = p * pt + k * CH
        return at + live

    total = lax.fori_loop(0, count, listed, 0)
    for k in range(GRP):
        sched_ref[total + k] = 0
    sched_ref[224] = (total + GRP - 1) // GRP


def best_matches(sched_ref, p_ref, q_ref, part_ref, best_ref):
    width = q_ref.shape[0]
    count = best_ref.shape[0]

    def step(g, _):
        rows = jnp.concatenate(
            [p_ref[pl.ds(pl.multiple_of(sched_ref[g * GRP + k], CH), CH), :] for k in range(GRP)],
            axis=0,
        )
        for c in range(width // COLS):
            sim = lax.dot_general(
                rows, q_ref[c * COLS : (c + 1) * COLS, :], NT, preferred_element_type=f32
            )
            m = jnp.max(sim.reshape(GRP, CH // 8, 8, COLS), axis=1)
            part_ref[pl.ds(pl.multiple_of(g * GRP * 8, GRP * 8), GRP * 8), c * COLS : (c + 1) * COLS] = (
                m.reshape(GRP * 8, COLS)
            )
        return 0

    lax.fori_loop(0, sched_ref[224], step, 0)

    def gather(p, _):
        at, live = sched_ref[160 + p], sched_ref[192 + p]
        m = None
        for k in range(256 // CH):
            c = at + jnp.minimum(k, live - 1)
            v = part_ref[pl.ds(pl.multiple_of(c * 8, 8), 8), :]
            m = v if m is None else jnp.maximum(m, v)
        best_ref[pl.ds(p, 1), :] = jnp.max(m, axis=0, keepdims=True)
        return 0

    lax.fori_loop(0, count, gather, 0)


def query_sums(best_ref):
    count, width = best_ref.shape
    nq = width // 32
    r = iota((nq, width), 0)
    member = jnp.where(iota((nq, width), 1) // 32 == (r & 7) * 8 + (r >> 3), 1.0, 0.0).astype(bf16)
    hi, lo = split2(best_ref[...])
    s = lax.dot_general(member, jnp.concatenate([hi, lo], axis=0), NT, preferred_element_type=f32)
    s = s[:, :count] + s[:, count:]
    return jnp.concatenate([s[k * 8 : k * 8 + 8] for k in range(nq // 8)], axis=1)


def first_kernel(sched_ref, p_ref, q_ref, t_ref, part_ref, best_ref):
    best_matches(sched_ref, p_ref, q_ref, part_ref, best_ref)
    t_ref[...] = query_sums(best_ref)


def second_kernel(sched_ref, core_ref, p_ref, q_ref, near_ref, o_ref, part_ref, best_ref):
    best_matches(sched_ref, p_ref, q_ref, part_ref, best_ref)
    near, far = near_ref[...], query_sums(best_ref)
    low = core_ref[0] == 0
    wide = jnp.concatenate([jnp.where(low, near, far), jnp.where(low, far, near)], axis=1)
    for g in range(o_ref.shape[1]):
        o_ref[:, g, :] = wide[:, g * 128 : (g + 1) * 128]


def final_kernel(count_ref, core_ref, cand_ref, near_ref, far_ref, o_ref):
    nq, nc = o_ref.shape
    rows = near_ref.shape[0]
    ids = jnp.concatenate([cand_ref[q : q + 1, :] for q in range(nq)], axis=1)
    owner, local = ids >> 5, ids & 31
    m = iota((rows, 1), 0)
    at = (m & 7) * 32 + (m >> 3) * 2
    step = 128 // nc
    out = []
    for g in range(nq // step):
        lanes = slice(g * 128, (g + 1) * 128)
        own, want = owner[:, lanes], local[:, lanes] + (iota((1, 128), 1) // nc) * 32
        x = None
        for ref, c in ((near_ref, core_ref[0]), (far_ref, 1 - core_ref[0])):
            hot = jnp.where(at + c == own, 1.0, 0.0).astype(bf16)
            for part in split2(ref[:, g, :]):
                y = lax.dot_general(part, hot, TN, preferred_element_type=f32)
                x = y if x is None else x + y
        out.append(jnp.sum(jnp.where(iota(x.shape, 0) == want, x, 0.0), axis=0, keepdims=True))
    for q in range(nq):
        row = out[q // step][:, (q % step) * nc : (q % step + 1) * nc]
        o_ref[q : q + 1, :] = row / count_ref[q].astype(f32)


def call(kernel, outs, ins, out_specs=VM, in_specs=None, scratch=()):
    return pl.pallas_call(
        kernel,
        out_shape=outs,
        in_specs=[VM] * len(ins) if in_specs is None else in_specs,
        out_specs=out_specs,
        scratch_shapes=scratch,
    )(*ins)


def body(
    query_fixed_encoding,
    passage_fde,
    query_tokens,
    query_token_totals,
    passage_tokens,
    passage_lengths,
    candidates,
):
    groups, shards = lax.axis_size("fde"), lax.axis_size("pas")
    nq, qt, dim = query_tokens.shape
    count, pt, _ = passage_tokens.shape
    core = lax.axis_index("pas") % 2
    swap = [(k, k ^ 1) for k in range(shards)]
    S = jax.ShapeDtypeStruct

    live = iota((nq, qt, dim), 1) < query_token_totals[:, None, None]
    mine = jnp.where(live, query_tokens, jnp.zeros((), bf16)).reshape(2, nq * qt // 2, dim)
    mine = lax.dynamic_index_in_dim(mine, core, 0, keepdims=False)
    tiles = jnp.broadcast_to(mine[None], (groups,) + mine.shape)
    near = lax.all_to_all(tiles, "fde", 0, 0, tiled=True)
    near = near.reshape(-1, dim)
    far = lax.ppermute(near, "pas", swap)

    clean, sched = call(
        prep_kernel,
        (S(passage_tokens.shape, bf16), S((256,), i32)),
        (passage_lengths, passage_tokens),
        (VM, SM),
        [SM, VM],
    )
    clean = clean.reshape(count * pt, dim)

    partial = lax.dot_general(
        query_fixed_encoding, passage_fde, NT, preferred_element_type=f32
    )
    tiles = lax.all_to_all(partial.reshape(groups, nq, -1), "fde", 0, 0, tiled=True)
    fde_scores = jnp.sum(tiles, axis=0)

    width = near.shape[0]
    scratch = [pltpu.VMEM((count * pt // CH * 8, width), f32), pltpu.VMEM((count, width), f32)]
    near_sums = call(
        first_kernel,
        S((groups, nq // 2 * count), f32),
        (sched, clean, near),
        VM,
        [SM, VM, VM],
        scratch,
    )
    sums = call(
        second_kernel,
        S((groups, nq * count // 128, 128), f32),
        (sched, core.reshape(1), clean, far, near_sums),
        VM,
        [SM, SM, VM, VM, VM],
        scratch,
    )
    mine = lax.all_to_all(sums, "fde", 0, 0, tiled=True)
    half = shards // 2
    near = lax.all_to_all(
        jnp.broadcast_to(mine[None], (half,) + mine.shape),
        "pas",
        0,
        0,
        axis_index_groups=[[2 * k + c for k in range(half)] for c in range(2)],
        tiled=True,
    ).reshape(half * groups, -1, 128)
    far = lax.ppermute(near, "pas", swap)
    rerank = call(
        final_kernel,
        S(candidates.shape, f32),
        (query_token_totals, core.reshape(1), candidates, near, far),
        VM,
        [SM, SM, VM, VM, VM],
    )
    return fde_scores, rerank


def solution(mesh):
    return jax.shard_map(
        body,
        mesh=mesh,
        in_specs=(
            P(None, "fde"),
            P("pas", "fde"),
            P("fde", None, None),
            P("fde"),
            P(("fde", "pas"), None, None),
            P(("fde", "pas")),
            P("fde", "pas"),
        ),
        out_specs=(P("fde", "pas"), P("fde", "pas")),
        check_vma=False,
    )
```

```python
import jax
import jax.numpy as jnp
from jax import lax
from jax.experimental import pallas as pl
from jax.experimental.pallas import tpu as pltpu
from jax.sharding import PartitionSpec as P


f32, bf16, i32 = jnp.float32, jnp.bfloat16, jnp.int32
NT = (((1,), (1,)), ((), ()))
TN = (((0,), (0,)), ((), ()))
VM = pl.BlockSpec(memory_space=pltpu.VMEM)
SM = pl.BlockSpec(memory_space=pltpu.SMEM)
CH = 64
GRP = 16
COLS = 256


def iota(shape, dim):
    return lax.broadcasted_iota(i32, shape, dim)


def split2(x):
    hi = x.astype(bf16)
    return hi, (x - hi.astype(f32)).astype(bf16)


def prep_kernel(len_ref, p_ref, o_ref, sched_ref):
    count, pt, dim = p_ref.shape
    per = pt // CH

    def clean(p, _):
        rows = p_ref[p].astype(f32)
        keep = iota((pt, dim), 0) < len_ref[p]
        o_ref[p] = jnp.where(keep, rows, rows[0:1, :]).astype(bf16)
        return 0

    lax.fori_loop(0, count, clean, 0, unroll=4)

    def listed(p, at):
        live = (len_ref[p] + (CH - 1)) // CH
        sched_ref[160 + p] = at
        sched_ref[192 + p] = live
        for k in range(per):
            sched_ref[at + k] = p * pt + k * CH
        return at + live

    total = lax.fori_loop(0, count, listed, 0)
    for k in range(GRP):
        sched_ref[total + k] = 0
    rest = total % GRP
    sched_ref[224] = total // GRP + jnp.where(rest > GRP // 2, 1, 0)
    sched_ref[225] = jnp.where((rest > 0) & (rest <= GRP // 2), 1, 0)


def best_matches(sched_ref, p_ref, q_ref, starts, part_ref, best_ref):
    count = best_ref.shape[0]

    def run(at, n):
        rows = jnp.concatenate(
            [p_ref[pl.ds(pl.multiple_of(sched_ref[at + k], CH), CH), :] for k in range(n)], axis=0
        )
        for c, start in enumerate(starts):
            sim = lax.dot_general(
                rows, q_ref[pl.ds(start, COLS), :], NT, preferred_element_type=f32
            )
            m = jnp.max(sim.reshape(n, CH // 8, 8, COLS), axis=1)
            part_ref[pl.ds(pl.multiple_of(at * 8, 64), n * 8), c * COLS : (c + 1) * COLS] = m.reshape(
                n * 8, COLS
            )

    def step(g, _):
        run(g * GRP, GRP)
        return 0

    full = sched_ref[224]
    lax.fori_loop(0, full, step, 0)

    @pl.when(sched_ref[225] == 1)
    def _():
        run(full * GRP, GRP // 2)

    def gather(p, _):
        at, live = sched_ref[160 + p], sched_ref[192 + p]
        m = None
        for k in range(256 // CH):
            c = at + jnp.minimum(k, live - 1)
            v = part_ref[pl.ds(pl.multiple_of(c * 8, 8), 8), :]
            m = v if m is None else jnp.maximum(m, v)
        best_ref[pl.ds(p, 1), :] = jnp.max(m, axis=0, keepdims=True)
        return 0

    lax.fori_loop(0, count, gather, 0, unroll=8)


def add_rows(member, best_ref):
    count = best_ref.shape[0]
    hi, lo = split2(best_ref[...])
    s = lax.dot_general(
        jnp.where(member, 1.0, 0.0).astype(bf16),
        jnp.concatenate([hi, lo], axis=0),
        NT,
        preferred_element_type=f32,
    )
    return s[:, :count] + s[:, count:]


def other_starts(pos_ref):
    return [pl.multiple_of(((pos_ref[0] + 1 + d) & 7) * COLS, COLS) for d in range(7)]


def query_sums(pos_ref, best_ref):
    shape = (64, best_ref.shape[1])
    r = iota(shape, 0)
    block = ((r & 7) - pos_ref[0] + 7) & 7
    s = add_rows(iota(shape, 1) // 32 == block * 8 + (r >> 3), best_ref)
    return jnp.concatenate([s[k * 8 : k * 8 + 8] for k in range(8)], axis=1)


def pack_kernel(pos_ref, count_ref, q_ref, all_ref, tiles_ref):
    nq, qt, dim = q_ref.shape

    def masked(q):
        keep = iota((qt, dim), 0) < count_ref[q]
        return jnp.where(keep, q_ref[q].astype(f32), 0.0).astype(bf16)

    for q in range(nq):
        all_ref[q * qt : (q + 1) * qt, :] = masked(q)
    for k in range(nq // 2):
        v = all_ref[pl.ds(pl.multiple_of((pos_ref[1] * (nq // 2) + k) * qt, qt), qt), :]
        for g in range(tiles_ref.shape[0]):
            tiles_ref[g, k * qt : (k + 1) * qt, :] = v


def own_kernel(sched_ref, pos_ref, p_ref, q_ref, t_ref, part_ref, best_ref):
    starts = range(0, q_ref.shape[0], COLS)
    best_matches(sched_ref, p_ref, q_ref, starts, part_ref, best_ref)
    shape = (q_ref.shape[0] // 32, q_ref.shape[0])
    s = add_rows(iota(shape, 1) // 32 == iota(shape, 0), best_ref)
    row = jnp.concatenate([s[q : q + 1] for q in range(shape[0])], axis=1)
    t_ref[...] = jnp.where(iota(t_ref.shape, 0) == pos_ref[0], row, 0.0)


def first_kernel(sched_ref, pos_ref, p_ref, q_ref, t_ref, part_ref, best_ref):
    best_matches(sched_ref, p_ref, q_ref, other_starts(pos_ref), part_ref, best_ref)
    t_ref[...] = query_sums(pos_ref, best_ref)


def second_kernel(sched_ref, pos_ref, p_ref, q_ref, own_ref, near_ref, o_ref, part_ref, best_ref):
    best_matches(sched_ref, p_ref, q_ref, other_starts(pos_ref), part_ref, best_ref)
    near, far = near_ref[...], query_sums(pos_ref, best_ref)
    low = pos_ref[1] == 0
    wide = jnp.concatenate([jnp.where(low, near, far), jnp.where(low, far, near)], axis=1)
    wide = wide + own_ref[...]
    for g in range(o_ref.shape[1]):
        o_ref[:, g, :] = wide[:, g * 128 : (g + 1) * 128]


def final_kernel(count_ref, pos_ref, cand_ref, near_ref, far_ref, o_ref):
    nq, nc = o_ref.shape
    rows, n = near_ref.shape[0], nq * nc
    ids = jnp.concatenate([cand_ref[q : q + 1, :] for q in range(nq)], axis=1)
    query = iota((1, n), 1) // nc
    want = (query & 3) * 32 + (ids & 31)
    key = (ids >> 5) * 4 + (query >> 2)
    r = iota((rows, 1), 0)
    at = ((r >> 2) & 7) * 128 + (r >> 5) * 8 + (r & 3)
    x = None
    for ref, c in ((near_ref, pos_ref[1]), (far_ref, 1 - pos_ref[1])):
        hot = jnp.where(at + c * 4 == key, 1.0, 0.0).astype(bf16)
        for part in split2(ref[...]):
            y = lax.dot_general(part, hot, TN, preferred_element_type=f32)
            x = y if x is None else x + y
    row = jnp.sum(jnp.where(iota(x.shape, 0) == want, x, 0.0), axis=0, keepdims=True)
    for q in range(nq):
        o_ref[q : q + 1, :] = row[:, q * nc : (q + 1) * nc] / count_ref[q].astype(f32)


def here(x):
    return pltpu.with_memory_space_constraint(x, pltpu.VMEM)


def call(kernel, outs, ins, out_specs=VM, in_specs=None, scratch=()):
    return pl.pallas_call(
        kernel,
        out_shape=outs,
        in_specs=[VM] * len(ins) if in_specs is None else in_specs,
        out_specs=out_specs,
        scratch_shapes=scratch,
        compiler_params=pltpu.CompilerParams(vmem_limit_bytes=20 << 20),
    )(*ins)


def body(
    query_fixed_encoding,
    passage_fde,
    query_tokens,
    query_token_totals,
    passage_tokens,
    passage_lengths,
    candidates,
):
    groups, shards = lax.axis_size("fde"), lax.axis_size("pas")
    nq, qt, dim = query_tokens.shape
    count, pt, _ = passage_tokens.shape
    core = lax.axis_index("pas") % 2
    swap = [(k, k ^ 1) for k in range(shards)]
    S = jax.ShapeDtypeStruct

    pos = jnp.stack([lax.axis_index("fde"), core])
    rows, tiles = call(
        pack_kernel,
        (pltpu.VMEM((nq * qt, dim), bf16), pltpu.VMEM((groups, nq * qt // 2, dim), bf16)),
        (pos, query_token_totals, query_tokens),
        (VM, VM),
        [SM, SM, VM],
    )
    near = lax.all_to_all(tiles, "fde", 0, 0, tiled=True)
    near = near.reshape(-1, dim)
    far = lax.ppermute(near, "pas", swap)

    clean, sched = call(
        prep_kernel,
        (pltpu.VMEM(passage_tokens.shape, bf16), S((256,), i32)),
        (passage_lengths, passage_tokens),
        (VM, SM),
        [SM, VM],
    )
    clean = clean.reshape(count * pt, dim)

    partial = lax.dot_general(
        query_fixed_encoding, passage_fde, NT, preferred_element_type=f32
    )
    tiles = lax.all_to_all(partial.reshape(groups, nq, -1), "fde", 0, 0, tiled=True)
    fde_scores = jnp.sum(tiles, axis=0)

    def scratch(width):
        return [pltpu.VMEM((count * pt // CH * 8, width), f32), pltpu.VMEM((count, width), f32)]

    own_sums = call(
        own_kernel,
        pltpu.VMEM((groups, nq * count), f32),
        (sched, pos, here(clean), here(rows)),
        VM,
        [SM, SM, VM, VM],
        scratch(nq * qt),
    )
    width = near.shape[0] - COLS
    near_sums = call(
        first_kernel,
        pltpu.VMEM((groups, nq // 2 * count), f32),
        (sched, pos, here(clean), here(near)),
        VM,
        [SM, SM, VM, VM],
        scratch(width),
    )
    sums = call(
        second_kernel,
        pltpu.VMEM((groups, nq * count // 128, 128), f32),
        (sched, pos, here(clean), here(far), here(own_sums), here(near_sums)),
        VM,
        [SM, SM, VM, VM, VM, VM],
        scratch(width),
    )
    mine = lax.all_to_all(sums, "fde", 0, 0, tiled=True)
    half = shards // 2
    near = lax.all_to_all(
        jnp.broadcast_to(mine[None], (half,) + mine.shape),
        "pas",
        0,
        0,
        axis_index_groups=[[2 * k + c for k in range(half)] for c in range(2)],
        tiled=True,
    ).reshape(-1, 128)
    far = lax.ppermute(near, "pas", swap)
    rerank = call(
        final_kernel,
        S(candidates.shape, f32),
        (query_token_totals, pos, candidates, here(near), here(far)),
        VM,
        [SM, SM, VM, VM, VM],
    )
    return fde_scores, rerank


def solution(mesh):
    return jax.shard_map(
        body,
        mesh=mesh,
        in_specs=(
            P(None, "fde"),
            P("pas", "fde"),
            P("fde", None, None),
            P("fde"),
            P(("fde", "pas"), None, None),
            P(("fde", "pas")),
            P("fde", "pas"),
        ),
        out_specs=(P("fde", "pas"), P("fde", "pas")),
        check_vma=False,
    )
```

```python
import jax
import jax.numpy as jnp
from jax import lax
from jax.experimental import pallas as pl
from jax.experimental.pallas import tpu as pltpu
from jax.sharding import PartitionSpec as P


f32, bf16, i32 = jnp.float32, jnp.bfloat16, jnp.int32
NT = (((1,), (1,)), ((), ()))
TN = (((0,), (0,)), ((), ()))
VM = pl.BlockSpec(memory_space=pltpu.VMEM)
SM = pl.BlockSpec(memory_space=pltpu.SMEM)
CH = 64
GRP = 16
COLS = 256


def iota(shape, dim):
    return lax.broadcasted_iota(i32, shape, dim)


def split2(x):
    hi = x.astype(bf16)
    return hi, (x - hi.astype(f32)).astype(bf16)


def prep_kernel(len_ref, p_ref, o_ref, sched_ref):
    count, pt, dim = p_ref.shape
    per = pt // CH

    def clean(p, _):
        rows = p_ref[p].astype(f32)
        keep = iota((pt, dim), 0) < len_ref[p]
        o_ref[p] = jnp.where(keep, rows, rows[0:1, :]).astype(bf16)
        return 0

    lax.fori_loop(0, count, clean, 0, unroll=4)

    def listed(p, at):
        live = (len_ref[p] + (CH - 1)) // CH
        sched_ref[160 + p] = at
        sched_ref[192 + p] = live
        for k in range(per):
            sched_ref[at + k] = p * pt + k * CH
        return at + live

    total = lax.fori_loop(0, count, listed, 0)
    for k in range(GRP):
        sched_ref[total + k] = 0
    rest = total % GRP
    sched_ref[224] = total // GRP + jnp.where(rest > GRP // 2, 1, 0)
    sched_ref[225] = jnp.where((rest > 0) & (rest <= GRP // 2), 1, 0)


def best_matches(sched_ref, p_ref, q_ref, starts, part_ref, best_ref):
    count = best_ref.shape[0]

    def run(at, n):
        rows = jnp.concatenate(
            [p_ref[pl.ds(pl.multiple_of(sched_ref[at + k], CH), CH), :] for k in range(n)], axis=0
        )
        for c, start in enumerate(starts):
            sim = lax.dot_general(
                rows, q_ref[pl.ds(start, COLS), :], NT, preferred_element_type=f32
            )
            m = jnp.max(sim.reshape(n, CH // 8, 8, COLS), axis=1)
            part_ref[pl.ds(pl.multiple_of(at * 8, 64), n * 8), c * COLS : (c + 1) * COLS] = m.reshape(
                n * 8, COLS
            )

    def step(g, _):
        run(g * GRP, GRP)
        return 0

    full = sched_ref[224]
    lax.fori_loop(0, full, step, 0)

    @pl.when(sched_ref[225] == 1)
    def _():
        run(full * GRP, GRP // 2)

    def gather(p, _):
        at, live = sched_ref[160 + p], sched_ref[192 + p]
        m = None
        for k in range(256 // CH):
            c = at + jnp.minimum(k, live - 1)
            v = part_ref[pl.ds(pl.multiple_of(c * 8, 8), 8), :]
            m = v if m is None else jnp.maximum(m, v)
        best_ref[pl.ds(p, 1), :] = jnp.max(m, axis=0, keepdims=True)
        return 0

    lax.fori_loop(0, count, gather, 0, unroll=8)


def add_rows(member, best_ref):
    count = best_ref.shape[0]
    hi, lo = split2(best_ref[...])
    s = lax.dot_general(
        jnp.where(member, 1.0, 0.0).astype(bf16),
        jnp.concatenate([hi, lo], axis=0),
        NT,
        preferred_element_type=f32,
    )
    return s[:, :count] + s[:, count:]


def other_starts(pos_ref):
    return [pl.multiple_of(((pos_ref[0] + 1 + d) & 7) * COLS, COLS) for d in range(7)]


def query_sums(pos_ref, best_ref):
    shape = (64, best_ref.shape[1])
    r = iota(shape, 0)
    block = ((r & 7) - pos_ref[0] + 7) & 7
    s = add_rows(iota(shape, 1) // 32 == block * 8 + (r >> 3), best_ref)
    return jnp.concatenate([s[k * 8 : k * 8 + 8] for k in range(8)], axis=1)


def pack_kernel(pos_ref, count_ref, q_ref, all_ref, tiles_ref):
    nq, qt, dim = q_ref.shape

    def masked(q):
        keep = iota((qt, dim), 0) < count_ref[q]
        return jnp.where(keep, q_ref[q].astype(f32), 0.0).astype(bf16)

    for q in range(nq):
        all_ref[q * qt : (q + 1) * qt, :] = masked(q)
    for k in range(nq // 2):
        v = all_ref[pl.ds(pl.multiple_of((pos_ref[1] * (nq // 2) + k) * qt, qt), qt), :]
        for g in range(tiles_ref.shape[0]):
            tiles_ref[g, k * qt : (k + 1) * qt, :] = v


def own_kernel(sched_ref, pos_ref, p_ref, q_ref, t_ref, part_ref, best_ref):
    starts = range(0, q_ref.shape[0], COLS)
    best_matches(sched_ref, p_ref, q_ref, starts, part_ref, best_ref)
    shape = (q_ref.shape[0] // 32, q_ref.shape[0])
    s = add_rows(iota(shape, 1) // 32 == iota(shape, 0), best_ref)
    row = jnp.concatenate([s[q : q + 1] for q in range(shape[0])], axis=1)
    t_ref[...] = jnp.where(iota(t_ref.shape, 0) == pos_ref[0], row, 0.0)


def first_kernel(sched_ref, pos_ref, p_ref, q_ref, t_ref, part_ref, best_ref):
    best_matches(sched_ref, p_ref, q_ref, other_starts(pos_ref), part_ref, best_ref)
    t_ref[...] = query_sums(pos_ref, best_ref)


def second_kernel(
    sched_ref, pos_ref, p_ref, q_ref, own_ref, near_ref, fde_ref, o_ref, part_ref, best_ref
):
    nq = fde_ref.shape[0] // o_ref.shape[0]
    for i in range(o_ref.shape[0]):
        for h in range(fde_ref.shape[1] // 128):
            o_ref[i, h * nq : (h + 1) * nq, :] = fde_ref[
                i * nq : (i + 1) * nq, h * 128 : (h + 1) * 128
            ]
        o_ref[i, 32:40, :] = jnp.zeros((8, 128), f32)
    best_matches(sched_ref, p_ref, q_ref, other_starts(pos_ref), part_ref, best_ref)
    near, far = near_ref[...], query_sums(pos_ref, best_ref)
    low = pos_ref[1] == 0
    wide = jnp.concatenate([jnp.where(low, near, far), jnp.where(low, far, near)], axis=1)
    wide = wide + own_ref[...]
    for g in range(wide.shape[1] // 128):
        o_ref[:, 32 + g, :] = wide[:, g * 128 : (g + 1) * 128]


def fold_kernel(x_ref, o_ref):
    nq, width = o_ref.shape
    for h in range(width // 128):
        x = x_ref[0, h * nq : (h + 1) * nq, :]
        for i in range(1, x_ref.shape[0]):
            x = x + x_ref[i, h * nq : (h + 1) * nq, :]
        o_ref[:, h * 128 : (h + 1) * 128] = x


def final_kernel(count_ref, pos_ref, cand_ref, near_ref, far_ref, o_ref):
    nq, nc = o_ref.shape
    rows, n = near_ref.shape[0], nq * nc
    ids = jnp.concatenate([cand_ref[q : q + 1, :] for q in range(nq)], axis=1)
    query = iota((1, n), 1) // nc
    want = (query & 3) * 32 + (ids & 31)
    key = (ids >> 5) * 4 + (query >> 2)
    r = iota((rows, 1), 0)
    at = ((r >> 2) & 7) * 128 + (r >> 5) * 8 + (r & 3)
    x = None
    for ref, c in ((near_ref, pos_ref[1]), (far_ref, 1 - pos_ref[1])):
        hot = jnp.where(at + c * 4 == key, 1.0, 0.0).astype(bf16)
        for part in split2(ref[...]):
            y = lax.dot_general(part, hot, TN, preferred_element_type=f32)
            x = y if x is None else x + y
    row = jnp.sum(jnp.where(iota(x.shape, 0) == want, x, 0.0), axis=0, keepdims=True)
    for q in range(nq):
        o_ref[q : q + 1, :] = row[:, q * nc : (q + 1) * nc] / count_ref[q].astype(f32)


def in_vmem(x):
    return pltpu.with_memory_space_constraint(x, pltpu.VMEM)


def in_hbm(x):
    return pltpu.with_memory_space_constraint(x, pltpu.HBM)


def call(kernel, outs, ins, out_specs=VM, in_specs=None, scratch=()):
    return pl.pallas_call(
        kernel,
        out_shape=outs,
        in_specs=[VM] * len(ins) if in_specs is None else in_specs,
        out_specs=out_specs,
        scratch_shapes=scratch,
        compiler_params=pltpu.CompilerParams(vmem_limit_bytes=20 << 20),
    )(*ins)


def body(
    query_fixed_encoding,
    passage_fde,
    query_tokens,
    query_token_totals,
    passage_tokens,
    passage_lengths,
    candidates,
):
    groups, shards = lax.axis_size("fde"), lax.axis_size("pas")
    nq, qt, dim = query_tokens.shape
    count, pt, _ = passage_tokens.shape
    core = lax.axis_index("pas") % 2
    swap = [(k, k ^ 1) for k in range(shards)]
    S = jax.ShapeDtypeStruct

    pos = in_hbm(jnp.stack([lax.axis_index("fde"), core]))
    rows, tiles = call(
        pack_kernel,
        (pltpu.VMEM((nq * qt, dim), bf16), pltpu.VMEM((groups, nq * qt // 2, dim), bf16)),
        (pos, in_hbm(query_token_totals), in_hbm(query_tokens)),
        (VM, VM),
        [SM, SM, VM],
    )
    near = lax.all_to_all(tiles, "fde", 0, 0, tiled=True)
    near = near.reshape(-1, dim)
    far = lax.ppermute(near, "pas", swap)

    clean, sched = call(
        prep_kernel,
        (pltpu.VMEM(passage_tokens.shape, bf16), S((256,), i32)),
        (in_hbm(passage_lengths), in_hbm(passage_tokens)),
        (VM, SM),
        [SM, VM],
    )
    clean, sched = clean.reshape(count * pt, dim), in_hbm(sched)

    partial = lax.dot_general(
        query_fixed_encoding, passage_fde, NT, preferred_element_type=f32
    )

    def scratch(width):
        return [pltpu.VMEM((count * pt // CH * 8, width), f32), pltpu.VMEM((count, width), f32)]

    own_sums = call(
        own_kernel,
        pltpu.VMEM((groups, nq * count), f32),
        (sched, pos, in_vmem(clean), in_vmem(rows)),
        VM,
        [SM, SM, VM, VM],
        scratch(nq * qt),
    )
    width = near.shape[0] - COLS
    near_sums = call(
        first_kernel,
        pltpu.VMEM((groups, nq // 2 * count), f32),
        (sched, pos, in_vmem(clean), in_vmem(near)),
        VM,
        [SM, SM, VM, VM],
        scratch(width),
    )
    sums = call(
        second_kernel,
        pltpu.VMEM((groups, 40, 128), f32),
        (sched, pos, in_vmem(clean), in_vmem(far), in_vmem(own_sums), in_vmem(near_sums), in_vmem(partial)),
        VM,
        [SM, SM, VM, VM, VM, VM, VM],
        scratch(width),
    )
    back = lax.all_to_all(sums, "fde", 0, 0, tiled=True)
    mine = back[:, 32 : 32 + nq * count // 128]
    fde_scores = call(fold_kernel, S((nq, passage_fde.shape[0]), f32), (in_vmem(back),))
    half = shards // 2
    near = lax.all_to_all(
        jnp.broadcast_to(mine[None], (half,) + mine.shape),
        "pas",
        0,
        0,
        axis_index_groups=[[2 * k + c for k in range(half)] for c in range(2)],
        tiled=True,
    ).reshape(-1, 128)
    far = lax.ppermute(near, "pas", swap)
    rerank = call(
        final_kernel,
        S(candidates.shape, f32),
        (in_hbm(query_token_totals), pos, in_hbm(candidates), in_vmem(near), in_vmem(far)),
        VM,
        [SM, SM, VM, VM, VM],
    )
    return fde_scores, rerank


def solution(mesh):
    return jax.shard_map(
        body,
        mesh=mesh,
        in_specs=(
            P(None, "fde"),
            P("pas", "fde"),
            P("fde", None, None),
            P("fde"),
            P(("fde", "pas"), None, None),
            P(("fde", "pas")),
            P("fde", "pas"),
        ),
        out_specs=(P("fde", "pas"), P("fde", "pas")),
        check_vma=False,
    )
```

```python
import jax
import jax.numpy as jnp
from jax import lax
from jax.experimental import pallas as pl
from jax.experimental.pallas import tpu as pltpu
from jax.sharding import PartitionSpec as P


f32, bf16, i32 = jnp.float32, jnp.bfloat16, jnp.int32
NT = (((1,), (1,)), ((), ()))
TN = (((0,), (0,)), ((), ()))
VM = pl.BlockSpec(memory_space=pltpu.VMEM)
SM = pl.BlockSpec(memory_space=pltpu.SMEM)
CH = 32
GRP = 32
COLS = 256


def iota(shape, dim):
    return lax.broadcasted_iota(i32, shape, dim)


def split2(x):
    hi = x.astype(bf16)
    return hi, (x - hi.astype(f32)).astype(bf16)


def prep_kernel(len_ref, p_ref, o_ref, sched_ref):
    count, pt, dim = p_ref.shape
    per = pt // CH

    def clean(p, _):
        rows = p_ref[p].astype(f32)
        keep = iota((pt, dim), 0) < len_ref[p]
        o_ref[p] = jnp.where(keep, rows, rows[0:1, :]).astype(bf16)
        return 0

    lax.fori_loop(0, count, clean, 0, unroll=4)

    def listed(p, at):
        live = (len_ref[p] + (CH - 1)) // CH
        sched_ref[320 + p] = at
        sched_ref[352 + p] = live
        for k in range(per):
            sched_ref[at + k] = p * pt + k * CH
        return at + live

    total = lax.fori_loop(0, count, listed, 0)
    for k in range(GRP):
        sched_ref[total + k] = 0
    rest = total % GRP
    sched_ref[384] = total // GRP + jnp.where(rest > GRP // 2, 1, 0)
    sched_ref[385] = jnp.where((rest > 0) & (rest <= GRP // 2), 1, 0)


def best_matches(sched_ref, p_ref, q_ref, starts, part_ref, best_ref):
    count = best_ref.shape[0]

    def run(at, n):
        rows = jnp.concatenate(
            [p_ref[pl.ds(pl.multiple_of(sched_ref[at + k], CH), CH), :] for k in range(n)], axis=0
        )
        for c, start in enumerate(starts):
            sim = lax.dot_general(
                rows, q_ref[pl.ds(start, COLS), :], NT, preferred_element_type=f32
            )
            m = jnp.max(sim.reshape(n, CH // 8, 8, COLS), axis=1)
            part_ref[pl.ds(pl.multiple_of(at * 8, 64), n * 8), c * COLS : (c + 1) * COLS] = m.reshape(
                n * 8, COLS
            )

    def step(g, _):
        run(g * GRP, GRP)
        return 0

    full = sched_ref[384]
    lax.fori_loop(0, full, step, 0)

    @pl.when(sched_ref[385] == 1)
    def _():
        run(full * GRP, GRP // 2)

    def gather(p, _):
        at, live = sched_ref[320 + p], sched_ref[352 + p]
        m = None
        for k in range(256 // CH):
            c = at + jnp.minimum(k, live - 1)
            v = part_ref[pl.ds(pl.multiple_of(c * 8, 8), 8), :]
            m = v if m is None else jnp.maximum(m, v)
        best_ref[pl.ds(p, 1), :] = jnp.max(m, axis=0, keepdims=True)
        return 0

    lax.fori_loop(0, count, gather, 0, unroll=8)


def add_rows(member, best_ref):
    count = best_ref.shape[0]
    hi, lo = split2(best_ref[...])
    s = lax.dot_general(
        jnp.where(member, 1.0, 0.0).astype(bf16),
        jnp.concatenate([hi, lo], axis=0),
        NT,
        preferred_element_type=f32,
    )
    return s[:, :count] + s[:, count:]


def other_starts():
    return [pl.multiple_of(((lax.axis_index("fde") + 1 + d) & 7) * COLS, COLS) for d in range(7)]


def query_sums(best_ref):
    shape = (64, best_ref.shape[1])
    r = iota(shape, 0)
    block = ((r & 7) - lax.axis_index("fde") + 7) & 7
    s = add_rows(iota(shape, 1) // 32 == block * 8 + (r >> 3), best_ref)
    return jnp.concatenate([s[k * 8 : k * 8 + 8] for k in range(8)], axis=1)


def pack_kernel(count_ref, q_ref, all_ref, tiles_ref):
    nq, qt, dim = q_ref.shape

    def masked(q):
        keep = iota((qt, dim), 0) < count_ref[q]
        return jnp.where(keep, q_ref[q].astype(f32), 0.0).astype(bf16)

    for q in range(nq):
        all_ref[q * qt : (q + 1) * qt, :] = masked(q)
    for k in range(nq // 2):
        v = all_ref[pl.ds(pl.multiple_of(((lax.axis_index("pas") & 1) * (nq // 2) + k) * qt, qt), qt), :]
        for g in range(tiles_ref.shape[0]):
            tiles_ref[g, k * qt : (k + 1) * qt, :] = v


def own_kernel(sched_ref, p_ref, q_ref, t_ref, part_ref, best_ref):
    starts = range(0, q_ref.shape[0], COLS)
    best_matches(sched_ref, p_ref, q_ref, starts, part_ref, best_ref)
    shape = (q_ref.shape[0] // 32, q_ref.shape[0])
    s = add_rows(iota(shape, 1) // 32 == iota(shape, 0), best_ref)
    row = jnp.concatenate([s[q : q + 1] for q in range(shape[0])], axis=1)
    t_ref[...] = jnp.where(iota(t_ref.shape, 0) == lax.axis_index("fde"), row, 0.0)


def first_kernel(sched_ref, p_ref, q_ref, t_ref, part_ref, best_ref):
    best_matches(sched_ref, p_ref, q_ref, other_starts(), part_ref, best_ref)
    t_ref[...] = query_sums(best_ref)


def second_kernel(
    sched_ref, p_ref, q_ref, own_ref, near_ref, fde_ref, o_ref, part_ref, best_ref
):
    nq = fde_ref.shape[0] // o_ref.shape[0]
    for i in range(o_ref.shape[0]):
        for h in range(fde_ref.shape[1] // 128):
            o_ref[i, h * nq : (h + 1) * nq, :] = fde_ref[
                i * nq : (i + 1) * nq, h * 128 : (h + 1) * 128
            ]
        o_ref[i, 32:40, :] = jnp.zeros((8, 128), f32)
    best_matches(sched_ref, p_ref, q_ref, other_starts(), part_ref, best_ref)
    near, far = near_ref[...], query_sums(best_ref)
    low = (lax.axis_index("pas") & 1) == 0
    wide = jnp.concatenate([jnp.where(low, near, far), jnp.where(low, far, near)], axis=1)
    wide = wide + own_ref[...]
    for g in range(wide.shape[1] // 128):
        o_ref[:, 32 + g, :] = wide[:, g * 128 : (g + 1) * 128]


def spread_kernel(x_ref, o_ref):
    mine = x_ref[:, 32 : 32 + o_ref.shape[2], :]
    for k in range(o_ref.shape[0]):
        o_ref[k] = mine


def fold_kernel(x_ref, o_ref):
    nq, width = o_ref.shape
    for h in range(width // 128):
        x = x_ref[0, h * nq : (h + 1) * nq, :]
        for i in range(1, x_ref.shape[0]):
            x = x + x_ref[i, h * nq : (h + 1) * nq, :]
        o_ref[:, h * 128 : (h + 1) * 128] = x


def plan_kernel(cand_ref, near_ref, far_ref, want_ref):
    nq, nc = cand_ref.shape
    rows, n = near_ref.shape
    ids = jnp.concatenate([cand_ref[q : q + 1, :] for q in range(nq)], axis=1)
    query = iota((1, n), 1) // nc
    want_ref[...] = jnp.broadcast_to((query & 3) * 32 + (ids & 31), want_ref.shape)
    key = (ids >> 5) * 4 + (query >> 2)
    r = iota((rows, 1), 0)
    at = ((r >> 2) & 7) * 128 + (r >> 5) * 8 + (r & 3)
    core = lax.axis_index("pas") & 1
    for ref, c in ((near_ref, core), (far_ref, 1 - core)):
        ref[...] = jnp.where(at + c * 4 == key, 1.0, 0.0).astype(bf16)


def final_kernel(count_ref, want_ref, hot_near_ref, hot_far_ref, near_ref, far_ref, o_ref):
    nq, nc = o_ref.shape
    x = None
    for ref, hot in ((near_ref, hot_near_ref), (far_ref, hot_far_ref)):
        for part in split2(ref[...]):
            y = lax.dot_general(part, hot[...], TN, preferred_element_type=f32)
            x = y if x is None else x + y
    want = want_ref[0:1, :]
    row = jnp.sum(jnp.where(iota(x.shape, 0) == want, x, 0.0), axis=0, keepdims=True)
    for q in range(nq):
        o_ref[q : q + 1, :] = row[:, q * nc : (q + 1) * nc] / count_ref[q].astype(f32)


def in_vmem(x):
    return pltpu.with_memory_space_constraint(x, pltpu.VMEM)


def in_hbm(x):
    return pltpu.with_memory_space_constraint(x, pltpu.HBM)


def call(kernel, outs, ins, out_specs=VM, in_specs=None, scratch=()):
    return pl.pallas_call(
        kernel,
        out_shape=outs,
        in_specs=[VM] * len(ins) if in_specs is None else in_specs,
        out_specs=out_specs,
        scratch_shapes=scratch,
        compiler_params=pltpu.CompilerParams(vmem_limit_bytes=20 << 20),
    )(*ins)


def body(
    query_fixed_encoding,
    passage_fde,
    query_tokens,
    query_token_totals,
    passage_tokens,
    passage_lengths,
    candidates,
):
    groups, shards = lax.axis_size("fde"), lax.axis_size("pas")
    nq, qt, dim = query_tokens.shape
    count, pt, _ = passage_tokens.shape
    swap = [(k, k ^ 1) for k in range(shards)]
    S = jax.ShapeDtypeStruct

    rows, tiles = call(
        pack_kernel,
        (pltpu.VMEM((nq * qt, dim), bf16), pltpu.VMEM((groups, nq * qt // 2, dim), bf16)),
        (in_hbm(query_token_totals), in_hbm(query_tokens)),
        (VM, VM),
        [SM, VM],
    )
    near = lax.all_to_all(tiles, "fde", 0, 0, tiled=True)
    near = near.reshape(-1, dim)
    far = lax.ppermute(near, "pas", swap)

    clean, sched = call(
        prep_kernel,
        (pltpu.VMEM(passage_tokens.shape, bf16), S((512,), i32)),
        (in_hbm(passage_lengths), in_hbm(passage_tokens)),
        (VM, SM),
        [SM, VM],
    )
    clean, sched = clean.reshape(count * pt, dim), in_hbm(sched)

    partial = lax.dot_general(
        query_fixed_encoding, passage_fde, NT, preferred_element_type=f32
    )
    pairs, flat = nq * candidates.shape[1], shards // 2 * groups * nq * count // 128
    hot = pltpu.VMEM((flat, pairs), bf16)
    hot_near, hot_far, want = call(
        plan_kernel, (hot, hot, pltpu.VMEM((8, pairs), i32)), (candidates,), (VM, VM, VM)
    )

    def scratch(width):
        return [pltpu.VMEM((count * pt // CH * 8, width), f32), pltpu.VMEM((count, width), f32)]

    own_sums = call(
        own_kernel,
        pltpu.VMEM((groups, nq * count), f32),
        (sched, in_vmem(clean), in_vmem(rows)),
        VM,
        [SM, VM, VM],
        scratch(nq * qt),
    )
    width = near.shape[0] - COLS
    near_sums = call(
        first_kernel,
        pltpu.VMEM((groups, nq // 2 * count), f32),
        (sched, in_vmem(clean), in_vmem(near)),
        VM,
        [SM, VM, VM],
        scratch(width),
    )
    sums = call(
        second_kernel,
        pltpu.VMEM((groups, 40, 128), f32),
        (sched, in_vmem(clean), in_vmem(far), in_vmem(own_sums), in_vmem(near_sums), in_vmem(partial)),
        VM,
        [SM, VM, VM, VM, VM, VM],
        scratch(width),
    )
    back = lax.all_to_all(sums, "fde", 0, 0, tiled=True)
    blocks = nq * count // 128
    copies = call(
        spread_kernel, pltpu.VMEM((shards // 2, groups, blocks, 128), f32), (in_vmem(back),)
    )
    fde_scores = call(fold_kernel, S((nq, passage_fde.shape[0]), f32), (in_vmem(back),))
    half = shards // 2
    near = lax.all_to_all(
        copies,
        "pas",
        0,
        0,
        axis_index_groups=[[2 * k + c for k in range(half)] for c in range(2)],
        tiled=True,
    ).reshape(-1, 128)
    far = lax.ppermute(near, "pas", swap)
    rerank = call(
        final_kernel,
        S(candidates.shape, f32),
        (
            in_hbm(query_token_totals),
            in_vmem(want),
            in_vmem(hot_near),
            in_vmem(hot_far),
            in_vmem(near),
            in_vmem(far),
        ),
        VM,
        [SM, VM, VM, VM, VM, VM],
    )
    return fde_scores, rerank


def solution(mesh):
    return jax.shard_map(
        body,
        mesh=mesh,
        in_specs=(
            P(None, "fde"),
            P("pas", "fde"),
            P("fde", None, None),
            P("fde"),
            P(("fde", "pas"), None, None),
            P(("fde", "pas")),
            P("fde", "pas"),
        ),
        out_specs=(P("fde", "pas"), P("fde", "pas")),
        check_vma=False,
    )
```

```python
import jax
import jax.numpy as jnp
from jax import lax
from jax.experimental import pallas as pl
from jax.experimental.pallas import tpu as pltpu
from jax.sharding import PartitionSpec as P


f32, bf16, i32 = jnp.float32, jnp.bfloat16, jnp.int32
NT = (((1,), (1,)), ((), ()))
TN = (((0,), (0,)), ((), ()))
VM = pl.BlockSpec(memory_space=pltpu.VMEM)
SM = pl.BlockSpec(memory_space=pltpu.SMEM)
CH = 32
GRP = 32
COLS = 256


def iota(shape, dim):
    return lax.broadcasted_iota(i32, shape, dim)


def split2(x):
    hi = x.astype(bf16)
    return hi, (x - hi.astype(f32)).astype(bf16)


def prep_kernel(len_ref, p_ref, o_ref, sched_ref):
    count, pt, dim = p_ref.shape
    per = pt // CH

    def clean(p, _):
        rows = p_ref[p].astype(f32)
        keep = iota((pt, dim), 0) < len_ref[p]
        o_ref[p] = jnp.where(keep, rows, rows[0:1, :]).astype(bf16)
        return 0

    lax.fori_loop(0, count, clean, 0, unroll=4)

    def listed(p, at):
        live = (len_ref[p] + (CH - 1)) // CH
        sched_ref[320 + p] = at
        sched_ref[352 + p] = live
        for k in range(per):
            sched_ref[at + k] = p * pt + k * CH
        return at + live

    total = lax.fori_loop(0, count, listed, 0)
    for k in range(GRP):
        sched_ref[total + k] = 0
    rest = total % GRP
    sched_ref[384] = total // GRP + jnp.where(rest > GRP // 2, 1, 0)
    sched_ref[385] = jnp.where((rest > 0) & (rest <= GRP // 2), 1, 0)


def best_matches(sched_ref, p_ref, blocks, part_ref, best_ref):
    count = best_ref.shape[0]

    def run(at, n):
        rows = jnp.concatenate(
            [p_ref[pl.ds(pl.multiple_of(sched_ref[at + k], CH), CH), :] for k in range(n)], axis=0
        )
        for c, block in enumerate(blocks):
            sim = lax.dot_general(rows, block(), NT, preferred_element_type=f32)
            m = jnp.max(sim.reshape(n, CH // 8, 8, COLS), axis=1)
            part_ref[pl.ds(pl.multiple_of(at * 8, 64), n * 8), c * COLS : (c + 1) * COLS] = m.reshape(
                n * 8, COLS
            )

    def step(g, _):
        run(g * GRP, GRP)
        return 0

    full = sched_ref[384]
    lax.fori_loop(0, full, step, 0)

    @pl.when(sched_ref[385] == 1)
    def _():
        run(full * GRP, GRP // 2)

    def gather(p, _):
        at, live = sched_ref[320 + p], sched_ref[352 + p]
        m = None
        for k in range(256 // CH):
            c = at + jnp.minimum(k, live - 1)
            v = part_ref[pl.ds(pl.multiple_of(c * 8, 8), 8), :]
            m = v if m is None else jnp.maximum(m, v)
        best_ref[pl.ds(p, 1), :] = jnp.max(m, axis=0, keepdims=True)
        return 0

    lax.fori_loop(0, count, gather, 0, unroll=8)


def add_rows(member, best_ref):
    count = best_ref.shape[0]
    hi, lo = split2(best_ref[...])
    s = lax.dot_general(
        jnp.where(member, 1.0, 0.0).astype(bf16),
        jnp.concatenate([hi, lo], axis=0),
        NT,
        preferred_element_type=f32,
    )
    return s[:, :count] + s[:, count:]


def other_groups(a_ref, b_ref):
    half = COLS // 2

    def block(d):
        at = pl.multiple_of(((lax.axis_index("fde") + 1 + d) & 7) * half, half)
        return lambda: jnp.concatenate([r[pl.ds(at, half), :] for r in (a_ref, b_ref)], axis=0)

    return [block(d) for d in range(7)]


def place():
    p = lax.axis_index("pas")
    return ((p >> 3) + (p >> 1)) & 1, p & 1


def query_sums(best_ref):
    shape = (64, best_ref.shape[1])
    r = iota(shape, 0)
    block = ((r & 7) - lax.axis_index("fde") + 7) & 7
    s = add_rows(iota(shape, 1) // 32 == block * 8 + (r >> 3), best_ref)
    return jnp.concatenate([s[k * 8 : k * 8 + 8] for k in range(8)], axis=1)


def pack_kernel(count_ref, q_ref, all_ref, tiles_ref):
    nq, qt, dim = q_ref.shape

    def masked(q):
        keep = iota((qt, dim), 0) < count_ref[q]
        return jnp.where(keep, q_ref[q].astype(f32), 0.0).astype(bf16)

    for q in range(nq):
        all_ref[q * qt : (q + 1) * qt, :] = masked(q)
    parity, core = place()
    for k in range(nq // 4):
        v = all_ref[pl.ds(pl.multiple_of(((parity * 2 + core) * (nq // 4) + k) * qt, qt), qt), :]
        for g in range(tiles_ref.shape[0]):
            tiles_ref[g, k * qt : (k + 1) * qt, :] = v


def own_kernel(sched_ref, p_ref, q_ref, t_ref, part_ref, best_ref):
    blocks = [lambda at=at: q_ref[at : at + COLS, :] for at in range(0, q_ref.shape[0], COLS)]
    best_matches(sched_ref, p_ref, blocks, part_ref, best_ref)
    shape = (q_ref.shape[0] // 32, q_ref.shape[0])
    s = add_rows(iota(shape, 1) // 32 == iota(shape, 0), best_ref)
    row = jnp.concatenate([s[q : q + 1] for q in range(shape[0])], axis=1)
    t_ref[...] = jnp.where(iota(t_ref.shape, 0) == lax.axis_index("fde"), row, 0.0)


def first_kernel(sched_ref, p_ref, a_ref, b_ref, t_ref, part_ref, best_ref):
    best_matches(sched_ref, p_ref, other_groups(a_ref, b_ref), part_ref, best_ref)
    t_ref[...] = query_sums(best_ref)


def second_kernel(
    sched_ref, p_ref, a_ref, b_ref, own_ref, near_ref, fde_ref, o_ref, part_ref, best_ref
):
    nq = fde_ref.shape[0] // o_ref.shape[0]
    for i in range(o_ref.shape[0]):
        for h in range(fde_ref.shape[1] // 128):
            o_ref[i, h * nq : (h + 1) * nq, :] = fde_ref[
                i * nq : (i + 1) * nq, h * 128 : (h + 1) * 128
            ]
        o_ref[i, 32:40, :] = jnp.zeros((8, 128), f32)
    best_matches(sched_ref, p_ref, other_groups(a_ref, b_ref), part_ref, best_ref)
    parity, core = place()

    def ordered(swap, a, b):
        return jnp.concatenate([jnp.where(swap, b, a), jnp.where(swap, a, b)], axis=1)

    near, far = (
        ordered(core == 1, t[:, :128], t[:, 128:]) for t in (near_ref[...], query_sums(best_ref))
    )
    wide = ordered(parity == 1, near, far)
    wide = wide + own_ref[...]
    for g in range(wide.shape[1] // 128):
        o_ref[:, 32 + g, :] = wide[:, g * 128 : (g + 1) * 128]


def spread_kernel(x_ref, o_ref):
    for g in range(o_ref.shape[1]):
        mine = x_ref[:, 32 + g, :]
        for k in range(o_ref.shape[0]):
            o_ref[k, g] = mine


def fold_kernel(x_ref, o_ref):
    nq, width = o_ref.shape
    for h in range(width // 128):
        x = x_ref[0, h * nq : (h + 1) * nq, :]
        for i in range(1, x_ref.shape[0]):
            x = x + x_ref[i, h * nq : (h + 1) * nq, :]
        o_ref[:, h * 128 : (h + 1) * 128] = x


def plan_kernel(cand_ref, near_ref, far_ref, want_ref):
    nq, nc = cand_ref.shape
    rows, n = near_ref.shape
    ids = jnp.concatenate([cand_ref[q : q + 1, :] for q in range(nq)], axis=1)
    query = iota((1, n), 1) // nc
    want_ref[...] = jnp.broadcast_to((query & 3) * 32 + (ids & 31), want_ref.shape)
    owner = ids >> 5
    r = iota((rows, 1), 0)
    at = (r & 7) * 32 + (r >> 3) * 2
    core = lax.axis_index("pas") & 1
    for ref, c in ((near_ref, core), (far_ref, 1 - core)):
        ref[...] = jnp.where(at + c == owner, 1.0, 0.0).astype(bf16)


def final_kernel(count_ref, want_ref, hot_near_ref, hot_far_ref, near_ref, far_ref, o_ref):
    nq, nc = o_ref.shape
    blocks = nq * nc // 128
    copies = near_ref.shape[0] // (blocks * 8)
    for g in range(blocks):
        lanes = slice(g * 128, (g + 1) * 128)
        x = None
        for ref, hot in ((near_ref, hot_near_ref), (far_ref, hot_far_ref)):
            table = jnp.concatenate(
                [ref[(k * blocks + g) * 8 : (k * blocks + g) * 8 + 8, :] for k in range(copies)], axis=0
            )
            both = jnp.concatenate(split2(table), axis=1)
            y = lax.dot_general(both, hot[:, lanes], TN, preferred_element_type=f32)
            x = y if x is None else x + y
        x = x[:128] + x[128:]
        want = want_ref[0:1, lanes]
        row = jnp.sum(jnp.where(iota(x.shape, 0) == want, x, 0.0), axis=0, keepdims=True)
        for j in range(128 // nc):
            q = g * (128 // nc) + j
            o_ref[q : q + 1, :] = row[:, j * nc : (j + 1) * nc] / count_ref[q].astype(f32)


def in_vmem(x):
    return pltpu.with_memory_space_constraint(x, pltpu.VMEM)


def in_hbm(x):
    return pltpu.with_memory_space_constraint(x, pltpu.HBM)


def call(kernel, outs, ins, out_specs=VM, in_specs=None, scratch=()):
    return pl.pallas_call(
        kernel,
        out_shape=outs,
        in_specs=[VM] * len(ins) if in_specs is None else in_specs,
        out_specs=out_specs,
        scratch_shapes=scratch,
        compiler_params=pltpu.CompilerParams(vmem_limit_bytes=20 << 20),
    )(*ins)


def body(
    query_fixed_encoding,
    passage_fde,
    query_tokens,
    query_token_totals,
    passage_tokens,
    passage_lengths,
    candidates,
):
    groups, shards = lax.axis_size("fde"), lax.axis_size("pas")
    nq, qt, dim = query_tokens.shape
    count, pt, _ = passage_tokens.shape
    S = jax.ShapeDtypeStruct

    rows, tiles = call(
        pack_kernel,
        (pltpu.VMEM((nq * qt, dim), bf16), pltpu.VMEM((groups, nq * qt // 4, dim), bf16)),
        (in_hbm(query_token_totals), in_hbm(query_tokens)),
        (VM, VM),
        [SM, VM],
    )
    near = lax.all_to_all(tiles, "fde", 0, 0, tiled=True)
    quarter = near.reshape(-1, dim)

    def moved(x, flip):
        return lax.ppermute(x, "pas", [(k, k ^ flip) for k in range(shards)])

    core_q = moved(quarter, 1)
    x_q, y_q = moved(quarter, 8), moved(quarter, 3)
    clean, sched = call(
        prep_kernel,
        (pltpu.VMEM(passage_tokens.shape, bf16), S((512,), i32)),
        (in_hbm(passage_lengths), in_hbm(passage_tokens)),
        (VM, SM),
        [SM, VM],
    )
    clean, sched = clean.reshape(count * pt, dim), in_hbm(sched)

    partial = lax.dot_general(
        query_fixed_encoding, passage_fde, NT, preferred_element_type=f32
    )
    pairs = nq * candidates.shape[1]
    hot = pltpu.VMEM((shards // 2 * groups, pairs), bf16)
    hot_near, hot_far, want = call(
        plan_kernel, (hot, hot, pltpu.VMEM((8, pairs), i32)), (candidates,), (VM, VM, VM)
    )

    def scratch(width):
        return [pltpu.VMEM((count * pt // CH * 8, width), f32), pltpu.VMEM((count, width), f32)]

    own_sums = call(
        own_kernel,
        pltpu.VMEM((groups, nq * count), f32),
        (sched, in_vmem(clean), in_vmem(rows)),
        VM,
        [SM, VM, VM],
        scratch(nq * qt),
    )
    width = (groups - 1) * COLS
    near_sums = call(
        first_kernel,
        pltpu.VMEM((groups, nq // 2 * count), f32),
        (sched, in_vmem(clean), in_vmem(quarter), in_vmem(core_q)),
        VM,
        [SM, VM, VM, VM],
        scratch(width),
    )
    sums = call(
        second_kernel,
        pltpu.VMEM((groups, 40, 128), f32),
        (
            sched,
            in_vmem(clean),
            in_vmem(x_q),
            in_vmem(y_q),
            in_vmem(own_sums),
            in_vmem(near_sums),
            in_vmem(partial),
        ),
        VM,
        [SM, VM, VM, VM, VM, VM, VM],
        scratch(width),
    )
    back = lax.all_to_all(sums, "fde", 0, 0, tiled=True)
    blocks = nq * count // 128
    copies = call(
        spread_kernel, pltpu.VMEM((shards // 2, blocks, groups, 128), f32), (in_vmem(back),)
    )
    fde_scores = call(fold_kernel, S((nq, passage_fde.shape[0]), f32), (in_vmem(back),))
    half = shards // 2
    near = lax.all_to_all(
        copies,
        "pas",
        0,
        0,
        axis_index_groups=[[2 * k + c for k in range(half)] for c in range(2)],
        tiled=True,
    ).reshape(-1, 128)
    far = moved(near, 1)
    rerank = call(
        final_kernel,
        S(candidates.shape, f32),
        (
            in_hbm(query_token_totals),
            in_vmem(want),
            in_vmem(hot_near),
            in_vmem(hot_far),
            in_vmem(near),
            in_vmem(far),
        ),
        VM,
        [SM, VM, VM, VM, VM, VM],
    )
    return fde_scores, rerank


def solution(mesh):
    return jax.shard_map(
        body,
        mesh=mesh,
        in_specs=(
            P(None, "fde"),
            P("pas", "fde"),
            P("fde", None, None),
            P("fde"),
            P(("fde", "pas"), None, None),
            P(("fde", "pas")),
            P("fde", "pas"),
        ),
        out_specs=(P("fde", "pas"), P("fde", "pas")),
        check_vma=False,
    )
```

```python
import jax
import jax.numpy as jnp
from jax import lax
from jax.experimental import pallas as pl
from jax.experimental.pallas import tpu as pltpu
from jax.sharding import PartitionSpec as P


f32, bf16, i32 = jnp.float32, jnp.bfloat16, jnp.int32
NT = (((1,), (1,)), ((), ()))
TN = (((0,), (0,)), ((), ()))
VM = pl.BlockSpec(memory_space=pltpu.VMEM)
SM = pl.BlockSpec(memory_space=pltpu.SMEM)
CH = 32
GRP = 32
COLS = 256


def iota(shape, dim):
    return lax.broadcasted_iota(i32, shape, dim)


def split2(x):
    hi = x.astype(bf16)
    return hi, (x - hi.astype(f32)).astype(bf16)


def prep_kernel(len_ref, p_ref, o_ref, sched_ref, sem):
    count, pt, dim = o_ref.shape
    per = pt // CH
    copy = pltpu.make_async_copy(p_ref, o_ref, sem)
    copy.start()

    def listed(p, at):
        live = (len_ref[p] + (CH - 1)) // CH
        sched_ref[320 + p] = at
        sched_ref[352 + p] = live
        for k in range(per):
            sched_ref[at + k] = p * pt + k * CH
        return at + live

    total = lax.fori_loop(0, count, listed, 0)
    for k in range(GRP):
        sched_ref[total + k] = 0
    rest = total % GRP
    sched_ref[384] = total // GRP + jnp.where(rest > GRP // 2, 1, 0)
    sched_ref[385] = jnp.where((rest > 0) & (rest <= GRP // 2), 1, 0)
    copy.wait()

    def clean(p, _):
        at = pl.multiple_of((len_ref[p] - 1) // CH * CH, CH)
        rows = o_ref[p, pl.ds(at, CH), :].astype(f32)
        first = o_ref[p, 0:CH, :].astype(f32)[0:1, :]
        keep = iota((CH, dim), 0) + at < len_ref[p]
        o_ref[p, pl.ds(at, CH), :] = jnp.where(keep, rows, first).astype(bf16)
        return 0

    lax.fori_loop(0, count, clean, 0, unroll=4)


def best_matches(sched_ref, p_ref, blocks, part_ref, best_ref):
    count = best_ref.shape[0]

    def run(at, n):
        rows = jnp.concatenate(
            [p_ref[pl.ds(pl.multiple_of(sched_ref[at + k], CH), CH), :] for k in range(n)], axis=0
        )
        for c, block in enumerate(blocks):
            sim = lax.dot_general(rows, block(), NT, preferred_element_type=f32)
            m = jnp.max(sim.reshape(n, CH // 8, 8, COLS), axis=1)
            part_ref[pl.ds(pl.multiple_of(at * 8, 64), n * 8), c * COLS : (c + 1) * COLS] = m.reshape(
                n * 8, COLS
            )

    def step(g, _):
        run(g * GRP, GRP)
        return 0

    full = sched_ref[384]
    lax.fori_loop(0, full, step, 0)

    @pl.when(sched_ref[385] == 1)
    def _():
        run(full * GRP, GRP // 2)

    def gather(p, _):
        at, live = sched_ref[320 + p], sched_ref[352 + p]
        m = None
        for k in range(256 // CH):
            c = at + jnp.minimum(k, live - 1)
            v = part_ref[pl.ds(pl.multiple_of(c * 8, 8), 8), :]
            m = v if m is None else jnp.maximum(m, v)
        best_ref[pl.ds(p, 1), :] = jnp.max(m, axis=0, keepdims=True)
        return 0

    lax.fori_loop(0, count, gather, 0, unroll=8)


def add_rows(member, best_ref):
    count = best_ref.shape[0]
    hi, lo = split2(best_ref[...])
    s = lax.dot_general(
        jnp.where(member, 1.0, 0.0).astype(bf16),
        jnp.concatenate([hi, lo], axis=0),
        NT,
        preferred_element_type=f32,
    )
    return s[:, :count] + s[:, count:]


def other_groups(a_ref, b_ref):
    half = COLS // 2

    def block(d):
        at = pl.multiple_of(((lax.axis_index("fde") + 1 + d) & 7) * half, half)
        return lambda: jnp.concatenate([r[pl.ds(at, half), :] for r in (a_ref, b_ref)], axis=0)

    return [block(d) for d in range(7)]


def place():
    p = lax.axis_index("pas")
    return ((p >> 3) + (p >> 1)) & 1, p & 1


def query_sums(best_ref):
    shape = (64, best_ref.shape[1])
    r = iota(shape, 0)
    block = ((r & 7) - lax.axis_index("fde") + 7) & 7
    s = add_rows(iota(shape, 1) // 32 == block * 8 + (r >> 3), best_ref)
    return jnp.concatenate([s[k * 8 : k * 8 + 8] for k in range(8)], axis=1)


def pack_kernel(count_ref, q_ref, all_ref, tiles_ref):
    nq, qt, dim = q_ref.shape

    def masked(q):
        keep = iota((qt, dim), 0) < count_ref[q]
        return jnp.where(keep, q_ref[q].astype(f32), 0.0).astype(bf16)

    for q in range(nq):
        all_ref[q * qt : (q + 1) * qt, :] = masked(q)
    parity, core = place()
    for k in range(nq // 4):
        v = all_ref[pl.ds(pl.multiple_of(((parity * 2 + core) * (nq // 4) + k) * qt, qt), qt), :]
        for g in range(tiles_ref.shape[0]):
            tiles_ref[g, k * qt : (k + 1) * qt, :] = v


def own_kernel(sched_ref, p_ref, q_ref, t_ref, part_ref, best_ref):
    blocks = [lambda at=at: q_ref[at : at + COLS, :] for at in range(0, q_ref.shape[0], COLS)]
    best_matches(sched_ref, p_ref, blocks, part_ref, best_ref)
    shape = (q_ref.shape[0] // 32, q_ref.shape[0])
    s = add_rows(iota(shape, 1) // 32 == iota(shape, 0), best_ref)
    row = jnp.concatenate([s[q : q + 1] for q in range(shape[0])], axis=1)
    t_ref[...] = jnp.where(iota(t_ref.shape, 0) == lax.axis_index("fde"), row, 0.0)


def first_kernel(sched_ref, p_ref, a_ref, b_ref, t_ref, part_ref, best_ref):
    best_matches(sched_ref, p_ref, other_groups(a_ref, b_ref), part_ref, best_ref)
    t_ref[...] = query_sums(best_ref)


def second_kernel(
    sched_ref, p_ref, a_ref, b_ref, own_ref, near_ref, fde_ref, o_ref, part_ref, best_ref
):
    nq = fde_ref.shape[0] // o_ref.shape[0]
    for i in range(o_ref.shape[0]):
        for h in range(fde_ref.shape[1] // 128):
            o_ref[i, h * nq : (h + 1) * nq, :] = fde_ref[
                i * nq : (i + 1) * nq, h * 128 : (h + 1) * 128
            ]
        o_ref[i, 32:40, :] = jnp.zeros((8, 128), f32)
    best_matches(sched_ref, p_ref, other_groups(a_ref, b_ref), part_ref, best_ref)
    parity, core = place()

    def ordered(swap, a, b):
        return jnp.concatenate([jnp.where(swap, b, a), jnp.where(swap, a, b)], axis=1)

    near, far = (
        ordered(core == 1, t[:, :128], t[:, 128:]) for t in (near_ref[...], query_sums(best_ref))
    )
    wide = ordered(parity == 1, near, far)
    wide = wide + own_ref[...]
    for g in range(wide.shape[1] // 128):
        o_ref[:, 32 + g, :] = wide[:, g * 128 : (g + 1) * 128]


def spread_kernel(x_ref, o_ref):
    for g in range(o_ref.shape[1]):
        mine = x_ref[:, 32 + g, :]
        for k in range(o_ref.shape[0]):
            o_ref[k, g] = mine


def fold_kernel(x_ref, o_ref):
    nq, width = o_ref.shape
    for h in range(width // 128):
        x = x_ref[0, h * nq : (h + 1) * nq, :]
        for i in range(1, x_ref.shape[0]):
            x = x + x_ref[i, h * nq : (h + 1) * nq, :]
        o_ref[:, h * 128 : (h + 1) * 128] = x


def plan_kernel(count_ref, cand_ref, near_ref, far_ref, want_ref, div_ref):
    nq, nc = cand_ref.shape
    rows, n = near_ref.shape
    ids = jnp.concatenate([cand_ref[q : q + 1, :] for q in range(nq)], axis=1)
    query = iota((1, n), 1) // nc
    want_ref[...] = jnp.broadcast_to((query & 3) * 32 + (ids & 31), want_ref.shape)
    div = jnp.zeros((1, n), f32)
    for q in range(nq):
        div = jnp.where(query == q, count_ref[q].astype(f32), div)
    div_ref[...] = jnp.broadcast_to(div, div_ref.shape)
    owner = ids >> 5
    r = iota((rows, 1), 0)
    at = (r & 7) * 32 + (r >> 3) * 2
    core = lax.axis_index("pas") & 1
    for ref, c in ((near_ref, core), (far_ref, 1 - core)):
        ref[...] = jnp.where(at + c == owner, 1.0, 0.0).astype(bf16)


def final_kernel(want_ref, div_ref, hot_near_ref, hot_far_ref, near_ref, far_ref, o_ref):
    nq, nc = o_ref.shape
    blocks = nq * nc // 128
    copies = near_ref.shape[0] // (blocks * 8)
    for g in range(blocks):
        lanes = slice(g * 128, (g + 1) * 128)
        x = None
        for ref, hot in ((near_ref, hot_near_ref), (far_ref, hot_far_ref)):
            table = jnp.concatenate(
                [ref[(k * blocks + g) * 8 : (k * blocks + g) * 8 + 8, :] for k in range(copies)], axis=0
            )
            both = jnp.concatenate(split2(table), axis=1)
            y = lax.dot_general(both, hot[:, lanes], TN, preferred_element_type=f32)
            x = y if x is None else x + y
        x = x[:128] + x[128:]
        want = want_ref[0:1, lanes]
        row = jnp.sum(jnp.where(iota(x.shape, 0) == want, x, 0.0), axis=0, keepdims=True)
        row = row / div_ref[0:1, lanes]
        for j in range(128 // nc):
            q = g * (128 // nc) + j
            o_ref[q : q + 1, :] = row[:, j * nc : (j + 1) * nc]


def in_vmem(x):
    return pltpu.with_memory_space_constraint(x, pltpu.VMEM)


def in_hbm(x):
    return pltpu.with_memory_space_constraint(x, pltpu.HBM)


def call(kernel, outs, ins, out_specs=VM, in_specs=None, scratch=()):
    return pl.pallas_call(
        kernel,
        out_shape=outs,
        in_specs=[VM] * len(ins) if in_specs is None else in_specs,
        out_specs=out_specs,
        scratch_shapes=scratch,
        compiler_params=pltpu.CompilerParams(vmem_limit_bytes=20 << 20),
    )(*ins)


def body(
    query_fixed_encoding,
    passage_fde,
    query_tokens,
    query_token_totals,
    passage_tokens,
    passage_lengths,
    candidates,
):
    groups, shards = lax.axis_size("fde"), lax.axis_size("pas")
    nq, qt, dim = query_tokens.shape
    count, pt, _ = passage_tokens.shape
    S = jax.ShapeDtypeStruct

    rows, tiles = call(
        pack_kernel,
        (pltpu.VMEM((nq * qt, dim), bf16), pltpu.VMEM((groups, nq * qt // 4, dim), bf16)),
        (in_hbm(query_token_totals), in_hbm(query_tokens)),
        (VM, VM),
        [SM, VM],
    )
    near = lax.all_to_all(tiles, "fde", 0, 0, tiled=True)
    quarter = near.reshape(-1, dim)

    def moved(x, flip):
        return lax.ppermute(x, "pas", [(k, k ^ flip) for k in range(shards)])

    core_q = moved(quarter, 1)
    x_q, y_q = moved(quarter, 8), moved(quarter, 3)
    clean, sched = call(
        prep_kernel,
        (pltpu.VMEM(passage_tokens.shape, bf16), pltpu.HBM((512,), i32)),
        (in_hbm(passage_lengths), in_hbm(passage_tokens)),
        (VM, SM),
        [SM, pl.BlockSpec(memory_space=pl.ANY)],
        [pltpu.SemaphoreType.DMA],
    )
    clean, sched = clean.reshape(count * pt, dim), in_hbm(sched)

    partial = lax.dot_general(
        query_fixed_encoding, passage_fde, NT, preferred_element_type=f32
    )
    pairs = nq * candidates.shape[1]
    hot = pltpu.VMEM((shards // 2 * groups, pairs), bf16)
    hot_near, hot_far, want, div = call(
        plan_kernel,
        (hot, hot, pltpu.VMEM((8, pairs), i32), pltpu.VMEM((8, pairs), f32)),
        (in_hbm(query_token_totals), candidates),
        (VM, VM, VM, VM),
        [SM, VM],
    )

    def scratch(width):
        return [pltpu.VMEM((count * pt // CH * 8, width), f32), pltpu.VMEM((count, width), f32)]

    own_sums = call(
        own_kernel,
        pltpu.VMEM((groups, nq * count), f32),
        (sched, in_vmem(clean), in_vmem(rows)),
        VM,
        [SM, VM, VM],
        scratch(nq * qt),
    )
    width = (groups - 1) * COLS
    near_sums = call(
        first_kernel,
        pltpu.VMEM((groups, nq // 2 * count), f32),
        (sched, in_vmem(clean), in_vmem(quarter), in_vmem(core_q)),
        VM,
        [SM, VM, VM, VM],
        scratch(width),
    )
    sums = call(
        second_kernel,
        pltpu.VMEM((groups, 40, 128), f32),
        (
            sched,
            in_vmem(clean),
            in_vmem(x_q),
            in_vmem(y_q),
            in_vmem(own_sums),
            in_vmem(near_sums),
            in_vmem(partial),
        ),
        VM,
        [SM, VM, VM, VM, VM, VM, VM],
        scratch(width),
    )
    back = lax.all_to_all(sums, "fde", 0, 0, tiled=True)
    blocks = nq * count // 128
    copies = call(
        spread_kernel, pltpu.VMEM((shards // 2, blocks, groups, 128), f32), (in_vmem(back),)
    )
    fde_scores = call(fold_kernel, S((nq, passage_fde.shape[0]), f32), (in_vmem(back),))
    half = shards // 2
    near = lax.all_to_all(
        copies,
        "pas",
        0,
        0,
        axis_index_groups=[[2 * k + c for k in range(half)] for c in range(2)],
        tiled=True,
    ).reshape(-1, 128)
    far = moved(near, 1)
    rerank = call(
        final_kernel,
        S(candidates.shape, f32),
        (
            in_vmem(want),
            in_vmem(div),
            in_vmem(hot_near),
            in_vmem(hot_far),
            in_vmem(near),
            in_vmem(far),
        ),
    )
    return fde_scores, rerank


def solution(mesh):
    return jax.shard_map(
        body,
        mesh=mesh,
        in_specs=(
            P(None, "fde"),
            P("pas", "fde"),
            P("fde", None, None),
            P("fde"),
            P(("fde", "pas"), None, None),
            P(("fde", "pas")),
            P("fde", "pas"),
        ),
        out_specs=(P("fde", "pas"), P("fde", "pas")),
        check_vma=False,
    )
```

```python
import jax
import jax.numpy as jnp
from jax import lax
from jax.experimental import pallas as pl
from jax.experimental.pallas import tpu as pltpu
from jax.sharding import PartitionSpec as P


f32, bf16, i32 = jnp.float32, jnp.bfloat16, jnp.int32
NT = (((1,), (1,)), ((), ()))
TN = (((0,), (0,)), ((), ()))
VM = pl.BlockSpec(memory_space=pltpu.VMEM)
SM = pl.BlockSpec(memory_space=pltpu.SMEM)
CH = 32
GRP = 64
COLS = 256


def iota(shape, dim):
    return lax.broadcasted_iota(i32, shape, dim)


def split2(x):
    hi = x.astype(bf16)
    return hi, (x - hi.astype(f32)).astype(bf16)


def prep_kernel(len_ref, p_ref, o_ref, sched_ref, sem):
    count, pt, dim = o_ref.shape
    per = pt // CH
    copy = pltpu.make_async_copy(p_ref, o_ref, sem)
    copy.start()

    def listed(p, at):
        live = (len_ref[p] + (CH - 1)) // CH
        sched_ref[320 + p] = at
        sched_ref[352 + p] = live
        for k in range(per):
            sched_ref[at + k] = p * pt + k * CH
        return at + live

    total = lax.fori_loop(0, count, listed, 0)
    for k in range(GRP):
        sched_ref[total + k] = 0
    rest = total % GRP
    sched_ref[384] = total // GRP + jnp.where(rest > GRP // 2, 1, 0)
    sched_ref[385] = jnp.where((rest > 0) & (rest <= GRP // 2), 1, 0)
    copy.wait()

    def clean(p, _):
        at = pl.multiple_of((len_ref[p] - 1) // CH * CH, CH)
        rows = o_ref[p, pl.ds(at, CH), :].astype(f32)
        first = o_ref[p, 0:CH, :].astype(f32)[0:1, :]
        keep = iota((CH, dim), 0) + at < len_ref[p]
        o_ref[p, pl.ds(at, CH), :] = jnp.where(keep, rows, first).astype(bf16)
        return 0

    lax.fori_loop(0, count, clean, 0, unroll=4)


def best_matches(sched_ref, p_ref, blocks, part_ref, best_ref):
    count = best_ref.shape[0]

    def run(at, n):
        rows = jnp.concatenate(
            [p_ref[pl.ds(pl.multiple_of(sched_ref[at + k], CH), CH), :] for k in range(n)], axis=0
        )
        for c, block in enumerate(blocks):
            sim = lax.dot_general(rows, block(), NT, preferred_element_type=f32)
            m = jnp.max(sim.reshape(n, CH // 8, 8, COLS), axis=1)
            part_ref[pl.ds(pl.multiple_of(at * 8, 64), n * 8), c * COLS : (c + 1) * COLS] = m.reshape(
                n * 8, COLS
            )

    def step(g, _):
        run(g * GRP, GRP)
        return 0

    full = sched_ref[384]
    lax.fori_loop(0, full, step, 0)

    @pl.when(sched_ref[385] == 1)
    def _():
        run(full * GRP, GRP // 2)

    def gather(p, _):
        at, live = sched_ref[320 + p], sched_ref[352 + p]
        m = None
        for k in range(256 // CH):
            c = at + jnp.minimum(k, live - 1)
            v = part_ref[pl.ds(pl.multiple_of(c * 8, 8), 8), :]
            m = v if m is None else jnp.maximum(m, v)
        best_ref[pl.ds(p, 1), :] = jnp.max(m, axis=0, keepdims=True)
        return 0

    lax.fori_loop(0, count, gather, 0, unroll=8)


def add_rows(member, best_ref):
    count = best_ref.shape[0]
    hi, lo = split2(best_ref[...])
    s = lax.dot_general(
        jnp.where(member, 1.0, 0.0).astype(bf16),
        jnp.concatenate([hi, lo], axis=0),
        NT,
        preferred_element_type=f32,
    )
    return s[:, :count] + s[:, count:]


def other_groups(a_ref, b_ref):
    half = COLS // 2

    def block(d):
        at = pl.multiple_of(((lax.axis_index("fde") + 1 + d) & 7) * half, half)
        return lambda: jnp.concatenate([r[pl.ds(at, half), :] for r in (a_ref, b_ref)], axis=0)

    return [block(d) for d in range(7)]


def place():
    p = lax.axis_index("pas")
    return ((p >> 3) + (p >> 1)) & 1, p & 1


def query_sums(best_ref):
    shape = (64, best_ref.shape[1])
    r = iota(shape, 0)
    block = ((r & 7) - lax.axis_index("fde") + 7) & 7
    s = add_rows(iota(shape, 1) // 32 == block * 8 + (r >> 3), best_ref)
    return jnp.concatenate([s[k * 8 : k * 8 + 8] for k in range(8)], axis=1)


def pack_kernel(count_ref, q_ref, all_ref, tiles_ref):
    nq, qt, dim = q_ref.shape

    def masked(q):
        keep = iota((qt, dim), 0) < count_ref[q]
        return jnp.where(keep, q_ref[q].astype(f32), 0.0).astype(bf16)

    for q in range(nq):
        all_ref[q * qt : (q + 1) * qt, :] = masked(q)
    parity, core = place()
    for k in range(nq // 4):
        v = all_ref[pl.ds(pl.multiple_of(((parity * 2 + core) * (nq // 4) + k) * qt, qt), qt), :]
        for g in range(tiles_ref.shape[0]):
            tiles_ref[g, k * qt : (k + 1) * qt, :] = v


def own_kernel(sched_ref, p_ref, q_ref, t_ref, part_ref, best_ref):
    blocks = [lambda at=at: q_ref[at : at + COLS, :] for at in range(0, q_ref.shape[0], COLS)]
    best_matches(sched_ref, p_ref, blocks, part_ref, best_ref)
    shape = (q_ref.shape[0] // 32, q_ref.shape[0])
    s = add_rows(iota(shape, 1) // 32 == iota(shape, 0), best_ref)
    row = jnp.concatenate([s[q : q + 1] for q in range(shape[0])], axis=1)
    t_ref[...] = jnp.where(iota(t_ref.shape, 0) == lax.axis_index("fde"), row, 0.0)


def first_kernel(sched_ref, p_ref, a_ref, b_ref, t_ref, part_ref, best_ref):
    best_matches(sched_ref, p_ref, other_groups(a_ref, b_ref), part_ref, best_ref)
    t_ref[...] = query_sums(best_ref)


def second_kernel(
    sched_ref, p_ref, a_ref, b_ref, own_ref, near_ref, fde_ref, o_ref, part_ref, best_ref
):
    nq = fde_ref.shape[0] // o_ref.shape[0]
    for i in range(o_ref.shape[0]):
        for h in range(fde_ref.shape[1] // 128):
            o_ref[i, h * nq : (h + 1) * nq, :] = fde_ref[
                i * nq : (i + 1) * nq, h * 128 : (h + 1) * 128
            ]
        o_ref[i, 32:40, :] = jnp.zeros((8, 128), f32)
    best_matches(sched_ref, p_ref, other_groups(a_ref, b_ref), part_ref, best_ref)
    parity, core = place()

    def ordered(swap, a, b):
        return jnp.concatenate([jnp.where(swap, b, a), jnp.where(swap, a, b)], axis=1)

    near, far = (
        ordered(core == 1, t[:, :128], t[:, 128:]) for t in (near_ref[...], query_sums(best_ref))
    )
    wide = ordered(parity == 1, near, far)
    wide = wide + own_ref[...]
    for g in range(wide.shape[1] // 128):
        o_ref[:, 32 + g, :] = wide[:, g * 128 : (g + 1) * 128]


def spread_kernel(x_ref, o_ref):
    for g in range(o_ref.shape[1]):
        mine = x_ref[:, 32 + g, :]
        for k in range(o_ref.shape[0]):
            o_ref[k, g] = mine


def plan_kernel(count_ref, cand_ref, x_ref, fde_ref, near_ref, far_ref, want_ref, div_ref):
    for h in range(fde_ref.shape[1] // 128):
        rows = slice(h * fde_ref.shape[0], (h + 1) * fde_ref.shape[0])
        total = x_ref[0, rows, :]
        for i in range(1, x_ref.shape[0]):
            total = total + x_ref[i, rows, :]
        fde_ref[:, h * 128 : (h + 1) * 128] = total
    nq, nc = cand_ref.shape
    rows, n = near_ref.shape
    ids = jnp.concatenate([cand_ref[q : q + 1, :] for q in range(nq)], axis=1)
    query = iota((1, n), 1) // nc
    want_ref[...] = jnp.broadcast_to((query & 3) * 32 + (ids & 31), want_ref.shape)
    div = jnp.zeros((1, n), f32)
    for q in range(nq):
        div = jnp.where(query == q, count_ref[q].astype(f32), div)
    div_ref[...] = jnp.broadcast_to(div, div_ref.shape)
    owner = ids >> 5
    r = iota((rows, 1), 0)
    at = (r & 7) * 32 + (r >> 3) * 2
    core = lax.axis_index("pas") & 1
    for ref, c in ((near_ref, core), (far_ref, 1 - core)):
        ref[...] = jnp.where(at + c == owner, 1.0, 0.0).astype(bf16)


def final_kernel(want_ref, div_ref, hot_near_ref, hot_far_ref, near_ref, far_ref, o_ref):
    nq, nc = o_ref.shape
    blocks = nq * nc // 128
    copies = near_ref.shape[0] // (blocks * 8)
    for g in range(blocks):
        lanes = slice(g * 128, (g + 1) * 128)
        x = None
        for ref, hot in ((near_ref, hot_near_ref), (far_ref, hot_far_ref)):
            table = jnp.concatenate(
                [ref[(k * blocks + g) * 8 : (k * blocks + g) * 8 + 8, :] for k in range(copies)], axis=0
            )
            both = jnp.concatenate(split2(table), axis=1)
            y = lax.dot_general(both, hot[:, lanes], TN, preferred_element_type=f32)
            x = y if x is None else x + y
        x = x[:128] + x[128:]
        want = want_ref[0:1, lanes]
        row = jnp.sum(jnp.where(iota(x.shape, 0) == want, x, 0.0), axis=0, keepdims=True)
        row = row / div_ref[0:1, lanes]
        for j in range(128 // nc):
            q = g * (128 // nc) + j
            o_ref[q : q + 1, :] = row[:, j * nc : (j + 1) * nc]


def in_vmem(x):
    return pltpu.with_memory_space_constraint(x, pltpu.VMEM)


def in_hbm(x):
    return pltpu.with_memory_space_constraint(x, pltpu.HBM)


def call(kernel, outs, ins, out_specs=VM, in_specs=None, scratch=()):
    return pl.pallas_call(
        kernel,
        out_shape=outs,
        in_specs=[VM] * len(ins) if in_specs is None else in_specs,
        out_specs=out_specs,
        scratch_shapes=scratch,
        compiler_params=pltpu.CompilerParams(vmem_limit_bytes=20 << 20),
    )(*ins)


def body(
    query_fixed_encoding,
    passage_fde,
    query_tokens,
    query_token_totals,
    passage_tokens,
    passage_lengths,
    candidates,
):
    groups, shards = lax.axis_size("fde"), lax.axis_size("pas")
    nq, qt, dim = query_tokens.shape
    count, pt, _ = passage_tokens.shape
    S = jax.ShapeDtypeStruct

    rows, tiles = call(
        pack_kernel,
        (pltpu.VMEM((nq * qt, dim), bf16), pltpu.VMEM((groups, nq * qt // 4, dim), bf16)),
        (in_hbm(query_token_totals), in_hbm(query_tokens)),
        (VM, VM),
        [SM, VM],
    )
    near = lax.all_to_all(tiles, "fde", 0, 0, tiled=True)
    quarter = near.reshape(-1, dim)

    def moved(x, flip):
        return lax.ppermute(x, "pas", [(k, k ^ flip) for k in range(shards)])

    core_q = moved(quarter, 1)
    x_q, y_q = moved(quarter, 8), moved(quarter, 3)
    clean, sched = call(
        prep_kernel,
        (pltpu.VMEM(passage_tokens.shape, bf16), pltpu.HBM((512,), i32)),
        (in_hbm(passage_lengths), in_hbm(passage_tokens)),
        (VM, SM),
        [SM, pl.BlockSpec(memory_space=pl.ANY)],
        [pltpu.SemaphoreType.DMA],
    )
    clean, sched = clean.reshape(count * pt, dim), in_hbm(sched)

    partial = lax.dot_general(
        query_fixed_encoding, passage_fde, NT, preferred_element_type=f32
    )
    pairs = nq * candidates.shape[1]
    hot = pltpu.VMEM((shards // 2 * groups, pairs), bf16)

    def scratch(width):
        return [pltpu.VMEM((count * pt // CH * 8, width), f32), pltpu.VMEM((count, width), f32)]

    own_sums = call(
        own_kernel,
        pltpu.VMEM((groups, nq * count), f32),
        (sched, in_vmem(clean), in_vmem(rows)),
        VM,
        [SM, VM, VM],
        scratch(nq * qt),
    )
    width = (groups - 1) * COLS
    near_sums = call(
        first_kernel,
        pltpu.VMEM((groups, nq // 2 * count), f32),
        (sched, in_vmem(clean), in_vmem(quarter), in_vmem(core_q)),
        VM,
        [SM, VM, VM, VM],
        scratch(width),
    )
    sums = call(
        second_kernel,
        pltpu.VMEM((groups, 40, 128), f32),
        (
            sched,
            in_vmem(clean),
            in_vmem(x_q),
            in_vmem(y_q),
            in_vmem(own_sums),
            in_vmem(near_sums),
            in_vmem(partial),
        ),
        VM,
        [SM, VM, VM, VM, VM, VM, VM],
        scratch(width),
    )
    back = lax.all_to_all(sums, "fde", 0, 0, tiled=True)
    blocks = nq * count // 128
    copies = call(
        spread_kernel, pltpu.VMEM((shards // 2, blocks, groups, 128), f32), (in_vmem(back),)
    )
    fde_scores, hot_near, hot_far, want, div = call(
        plan_kernel,
        (
            S((nq, passage_fde.shape[0]), f32),
            hot,
            hot,
            pltpu.VMEM((8, pairs), i32),
            pltpu.VMEM((8, pairs), f32),
        ),
        (in_hbm(query_token_totals), candidates, in_vmem(back)),
        (VM, VM, VM, VM, VM),
        [SM, VM, VM],
    )
    half = shards // 2
    near = lax.all_to_all(
        copies,
        "pas",
        0,
        0,
        axis_index_groups=[[2 * k + c for k in range(half)] for c in range(2)],
        tiled=True,
    ).reshape(-1, 128)
    far = moved(near, 1)
    rerank = call(
        final_kernel,
        S(candidates.shape, f32),
        (
            in_vmem(want),
            in_vmem(div),
            in_vmem(hot_near),
            in_vmem(hot_far),
            in_vmem(near),
            in_vmem(far),
        ),
    )
    return fde_scores, rerank


def solution(mesh):
    return jax.shard_map(
        body,
        mesh=mesh,
        in_specs=(
            P(None, "fde"),
            P("pas", "fde"),
            P("fde", None, None),
            P("fde"),
            P(("fde", "pas"), None, None),
            P(("fde", "pas")),
            P("fde", "pas"),
        ),
        out_specs=(P("fde", "pas"), P("fde", "pas")),
        check_vma=False,
    )
```

```python
import jax
import jax.numpy as jnp
from jax import lax
from jax.experimental import pallas as pl
from jax.experimental.pallas import tpu as pltpu
from jax.sharding import PartitionSpec as P


f32, bf16, i32 = jnp.float32, jnp.bfloat16, jnp.int32
NT = (((1,), (1,)), ((), ()))
TN = (((0,), (0,)), ((), ()))
VM = pl.BlockSpec(memory_space=pltpu.VMEM)
SM = pl.BlockSpec(memory_space=pltpu.SMEM)
CH = 32
GRP = 64
COLS = 256


def iota(shape, dim):
    return lax.broadcasted_iota(i32, shape, dim)


def split2(x):
    hi = x.astype(bf16)
    return hi, (x - hi.astype(f32)).astype(bf16)


def prep_kernel(len_ref, p_ref, o_ref, sched_ref, sem):
    count, pt, dim = o_ref.shape
    per = pt // CH
    copy = pltpu.make_async_copy(p_ref, o_ref, sem)
    copy.start()

    def listed(p, at):
        live = (len_ref[p] + (CH - 1)) // CH
        sched_ref[320 + p] = at
        sched_ref[352 + p] = live
        for k in range(per):
            sched_ref[at + k] = p * pt + k * CH
        return at + live

    total = lax.fori_loop(0, count, listed, 0)
    for k in range(GRP):
        sched_ref[total + k] = 0
    rest = total % GRP
    quarters = (rest + (GRP // 4 - 1)) // (GRP // 4)
    sched_ref[384] = total // GRP + quarters // 4
    sched_ref[385] = quarters % 4
    copy.wait()

    def clean(p, _):
        at = pl.multiple_of((len_ref[p] - 1) // CH * CH, CH)
        rows = o_ref[p, pl.ds(at, CH), :].astype(f32)
        first = o_ref[p, 0:CH, :].astype(f32)[0:1, :]
        keep = iota((CH, dim), 0) + at < len_ref[p]
        o_ref[p, pl.ds(at, CH), :] = jnp.where(keep, rows, first).astype(bf16)
        return 0

    lax.fori_loop(0, count, clean, 0, unroll=4)


def best_matches(sched_ref, p_ref, blocks, part_ref, best_ref):
    count = best_ref.shape[0]

    def run(at, n):
        rows = jnp.concatenate(
            [p_ref[pl.ds(pl.multiple_of(sched_ref[at + k], CH), CH), :] for k in range(n)], axis=0
        )
        for c, block in enumerate(blocks):
            sim = lax.dot_general(rows, block(), NT, preferred_element_type=f32)
            m = jnp.max(sim.reshape(n, CH // 8, 8, COLS), axis=1)
            part_ref[pl.ds(pl.multiple_of(at * 8, 64), n * 8), c * COLS : (c + 1) * COLS] = m.reshape(
                n * 8, COLS
            )

    def step(g, _):
        run(g * GRP, GRP)
        return 0

    full = sched_ref[384]
    lax.fori_loop(0, full, step, 0)

    tail = sched_ref[385]

    @pl.when(tail >= 2)
    def _():
        run(full * GRP, GRP // 2)

    @pl.when(tail % 2 == 1)
    def _():
        run(full * GRP + (tail // 2) * (GRP // 2), GRP // 4)

    def gather(p, _):
        at, live = sched_ref[320 + p], sched_ref[352 + p]
        m = None
        for k in range(256 // CH):
            c = at + jnp.minimum(k, live - 1)
            v = part_ref[pl.ds(pl.multiple_of(c * 8, 8), 8), :]
            m = v if m is None else jnp.maximum(m, v)
        best_ref[pl.ds(p, 1), :] = jnp.max(m, axis=0, keepdims=True)
        return 0

    lax.fori_loop(0, count, gather, 0, unroll=32)


def add_rows(member, best_ref):
    count = best_ref.shape[0]
    hi, lo = split2(best_ref[...])
    s = lax.dot_general(
        jnp.where(member, 1.0, 0.0).astype(bf16),
        jnp.concatenate([hi, lo], axis=0),
        NT,
        preferred_element_type=f32,
    )
    return s[:, :count] + s[:, count:]


def other_groups(a_ref, b_ref):
    half = COLS // 2

    def block(d):
        at = pl.multiple_of(((lax.axis_index("fde") + 1 + d) & 7) * half, half)
        return lambda: jnp.concatenate([r[pl.ds(at, half), :] for r in (a_ref, b_ref)], axis=0)

    return [block(d) for d in range(7)]


def place():
    p = lax.axis_index("pas")
    return ((p >> 3) + (p >> 1)) & 1, p & 1


def query_sums(best_ref):
    shape = (64, best_ref.shape[1])
    r = iota(shape, 0)
    block = ((r & 7) - lax.axis_index("fde") + 7) & 7
    s = add_rows(iota(shape, 1) // 32 == block * 8 + (r >> 3), best_ref)
    return jnp.concatenate([s[k * 8 : k * 8 + 8] for k in range(8)], axis=1)


def pack_kernel(count_ref, q_ref, all_ref, tiles_ref):
    nq, qt, dim = q_ref.shape

    def masked(q):
        keep = iota((qt, dim), 0) < count_ref[q]
        return jnp.where(keep, q_ref[q].astype(f32), 0.0).astype(bf16)

    for q in range(nq):
        all_ref[q * qt : (q + 1) * qt, :] = masked(q)
    parity, core = place()
    for k in range(nq // 4):
        v = all_ref[pl.ds(pl.multiple_of(((parity * 2 + core) * (nq // 4) + k) * qt, qt), qt), :]
        for g in range(tiles_ref.shape[0]):
            tiles_ref[g, k * qt : (k + 1) * qt, :] = v


def own_kernel(sched_ref, p_ref, q_ref, t_ref, part_ref, best_ref):
    blocks = [lambda at=at: q_ref[at : at + COLS, :] for at in range(0, q_ref.shape[0], COLS)]
    best_matches(sched_ref, p_ref, blocks, part_ref, best_ref)
    shape = (q_ref.shape[0] // 32, q_ref.shape[0])
    s = add_rows(iota(shape, 1) // 32 == iota(shape, 0), best_ref)
    row = jnp.concatenate([s[q : q + 1] for q in range(shape[0])], axis=1)
    t_ref[...] = jnp.where(iota(t_ref.shape, 0) == lax.axis_index("fde"), row, 0.0)


def first_kernel(sched_ref, p_ref, a_ref, b_ref, t_ref, part_ref, best_ref):
    best_matches(sched_ref, p_ref, other_groups(a_ref, b_ref), part_ref, best_ref)
    t_ref[...] = query_sums(best_ref)


def second_kernel(
    sched_ref, p_ref, a_ref, b_ref, own_ref, near_ref, fde_ref, o_ref, part_ref, best_ref
):
    nq = fde_ref.shape[0] // o_ref.shape[0]
    for i in range(o_ref.shape[0]):
        for h in range(fde_ref.shape[1] // 128):
            o_ref[i, h * nq : (h + 1) * nq, :] = fde_ref[
                i * nq : (i + 1) * nq, h * 128 : (h + 1) * 128
            ]
        o_ref[i, 32:40, :] = jnp.zeros((8, 128), f32)
    best_matches(sched_ref, p_ref, other_groups(a_ref, b_ref), part_ref, best_ref)
    parity, core = place()

    def ordered(swap, a, b):
        return jnp.concatenate([jnp.where(swap, b, a), jnp.where(swap, a, b)], axis=1)

    near, far = (
        ordered(core == 1, t[:, :128], t[:, 128:]) for t in (near_ref[...], query_sums(best_ref))
    )
    wide = ordered(parity == 1, near, far)
    wide = wide + own_ref[...]
    for g in range(wide.shape[1] // 128):
        o_ref[:, 32 + g, :] = wide[:, g * 128 : (g + 1) * 128]


def spread_kernel(x_ref, o_ref):
    for g in range(o_ref.shape[1]):
        mine = x_ref[:, 32 + g, :]
        for k in range(o_ref.shape[0]):
            o_ref[k, g] = mine


def plan_kernel(count_ref, cand_ref, x_ref, fde_ref, near_ref, far_ref, want_ref, div_ref):
    for h in range(fde_ref.shape[1] // 128):
        rows = slice(h * fde_ref.shape[0], (h + 1) * fde_ref.shape[0])
        total = x_ref[0, rows, :]
        for i in range(1, x_ref.shape[0]):
            total = total + x_ref[i, rows, :]
        fde_ref[:, h * 128 : (h + 1) * 128] = total
    nq, nc = cand_ref.shape
    rows, n = near_ref.shape
    ids = jnp.concatenate([cand_ref[q : q + 1, :] for q in range(nq)], axis=1)
    query = iota((1, n), 1) // nc
    want_ref[...] = jnp.broadcast_to((query & 3) * 32 + (ids & 31), want_ref.shape)
    div = jnp.zeros((1, n), f32)
    for q in range(nq):
        div = jnp.where(query == q, count_ref[q].astype(f32), div)
    div_ref[...] = jnp.broadcast_to(div, div_ref.shape)
    owner = ids >> 5
    r = iota((rows, 1), 0)
    at = (r & 7) * 32 + (r >> 3) * 2
    core = lax.axis_index("pas") & 1
    for ref, c in ((near_ref, core), (far_ref, 1 - core)):
        ref[...] = jnp.where(at + c == owner, 1.0, 0.0).astype(bf16)


def final_kernel(want_ref, div_ref, hot_near_ref, hot_far_ref, near_ref, far_ref, o_ref):
    nq, nc = o_ref.shape
    blocks = nq * nc // 128
    copies = near_ref.shape[0] // (blocks * 8)
    for g in range(blocks):
        lanes = slice(g * 128, (g + 1) * 128)
        x = None
        for ref, hot in ((near_ref, hot_near_ref), (far_ref, hot_far_ref)):
            table = jnp.concatenate(
                [ref[(k * blocks + g) * 8 : (k * blocks + g) * 8 + 8, :] for k in range(copies)], axis=0
            )
            both = jnp.concatenate(split2(table), axis=1)
            y = lax.dot_general(both, hot[:, lanes], TN, preferred_element_type=f32)
            x = y if x is None else x + y
        x = x[:128] + x[128:]
        want = want_ref[0:1, lanes]
        row = jnp.sum(jnp.where(iota(x.shape, 0) == want, x, 0.0), axis=0, keepdims=True)
        row = row / div_ref[0:1, lanes]
        for j in range(128 // nc):
            q = g * (128 // nc) + j
            o_ref[q : q + 1, :] = row[:, j * nc : (j + 1) * nc]


def in_vmem(x):
    return pltpu.with_memory_space_constraint(x, pltpu.VMEM)


def in_hbm(x):
    return pltpu.with_memory_space_constraint(x, pltpu.HBM)


def call(kernel, outs, ins, out_specs=VM, in_specs=None, scratch=()):
    return pl.pallas_call(
        kernel,
        out_shape=outs,
        in_specs=[VM] * len(ins) if in_specs is None else in_specs,
        out_specs=out_specs,
        scratch_shapes=scratch,
        compiler_params=pltpu.CompilerParams(vmem_limit_bytes=20 << 20),
    )(*ins)


def body(
    query_fixed_encoding,
    passage_fde,
    query_tokens,
    query_token_totals,
    passage_tokens,
    passage_lengths,
    candidates,
):
    groups, shards = lax.axis_size("fde"), lax.axis_size("pas")
    nq, qt, dim = query_tokens.shape
    count, pt, _ = passage_tokens.shape
    S = jax.ShapeDtypeStruct

    rows, tiles = call(
        pack_kernel,
        (pltpu.VMEM((nq * qt, dim), bf16), pltpu.VMEM((groups, nq * qt // 4, dim), bf16)),
        (in_hbm(query_token_totals), in_hbm(query_tokens)),
        (VM, VM),
        [SM, VM],
    )
    near = lax.all_to_all(tiles, "fde", 0, 0, tiled=True)
    quarter = near.reshape(-1, dim)

    def moved(x, flip):
        return lax.ppermute(x, "pas", [(k, k ^ flip) for k in range(shards)])

    core_q = moved(quarter, 1)
    x_q, y_q = moved(quarter, 8), moved(quarter, 3)
    clean, sched = call(
        prep_kernel,
        (pltpu.VMEM(passage_tokens.shape, bf16), pltpu.HBM((512,), i32)),
        (in_hbm(passage_lengths), in_hbm(passage_tokens)),
        (VM, SM),
        [SM, pl.BlockSpec(memory_space=pl.ANY)],
        [pltpu.SemaphoreType.DMA],
    )
    clean, sched = clean.reshape(count * pt, dim), in_hbm(sched)

    partial = lax.dot_general(
        query_fixed_encoding, passage_fde, NT, preferred_element_type=f32
    )
    pairs = nq * candidates.shape[1]
    hot = pltpu.VMEM((shards // 2 * groups, pairs), bf16)

    def scratch(width):
        return [pltpu.VMEM((count * pt // CH * 8, width), f32), pltpu.VMEM((count, width), f32)]

    own_sums = call(
        own_kernel,
        pltpu.VMEM((groups, nq * count), f32),
        (sched, in_vmem(clean), in_vmem(rows)),
        VM,
        [SM, VM, VM],
        scratch(nq * qt),
    )
    width = (groups - 1) * COLS
    near_sums = call(
        first_kernel,
        pltpu.VMEM((groups, nq // 2 * count), f32),
        (sched, in_vmem(clean), in_vmem(quarter), in_vmem(core_q)),
        VM,
        [SM, VM, VM, VM],
        scratch(width),
    )
    sums = call(
        second_kernel,
        pltpu.VMEM((groups, 40, 128), f32),
        (
            sched,
            in_vmem(clean),
            in_vmem(x_q),
            in_vmem(y_q),
            in_vmem(own_sums),
            in_vmem(near_sums),
            in_vmem(partial),
        ),
        VM,
        [SM, VM, VM, VM, VM, VM, VM],
        scratch(width),
    )
    back = lax.all_to_all(sums, "fde", 0, 0, tiled=True)
    blocks = nq * count // 128
    copies = call(
        spread_kernel, pltpu.VMEM((shards // 2, blocks, groups, 128), f32), (in_vmem(back),)
    )
    fde_scores, hot_near, hot_far, want, div = call(
        plan_kernel,
        (
            S((nq, passage_fde.shape[0]), f32),
            hot,
            hot,
            pltpu.VMEM((8, pairs), i32),
            pltpu.VMEM((8, pairs), f32),
        ),
        (in_hbm(query_token_totals), candidates, in_vmem(back)),
        (VM, VM, VM, VM, VM),
        [SM, VM, VM],
    )
    half = shards // 2
    near = lax.all_to_all(
        copies,
        "pas",
        0,
        0,
        axis_index_groups=[[2 * k + c for k in range(half)] for c in range(2)],
        tiled=True,
    ).reshape(-1, 128)
    far = moved(near, 1)
    rerank = call(
        final_kernel,
        S(candidates.shape, f32),
        (
            in_vmem(want),
            in_vmem(div),
            in_vmem(hot_near),
            in_vmem(hot_far),
            in_vmem(near),
            in_vmem(far),
        ),
    )
    return fde_scores, rerank


def solution(mesh):
    return jax.shard_map(
        body,
        mesh=mesh,
        in_specs=(
            P(None, "fde"),
            P("pas", "fde"),
            P("fde", None, None),
            P("fde"),
            P(("fde", "pas"), None, None),
            P(("fde", "pas")),
            P("fde", "pas"),
        ),
        out_specs=(P("fde", "pas"), P("fde", "pas")),
        check_vma=False,
    )
```
